32 devices in a mesh: dp: 8 (over y, x, core), tensor: 4 (over z).
Axes of the slice: x: 2, y: 2, z: 4, core: 2. Of those that a mesh axis runs over, the one named last changes fastest.
Arguments:
- queries: bfloat16 [2048, 3072], P('dp', 'tensor'), may hold values from -96 to 96
- keys: bfloat16 [2048, 512], P('dp'), may hold values from -6 to 6
- values: bfloat16 [2048, 512], P('dp'), may hold values from -6 to 6
- lengths: int32 [4], replicated, may hold values from 1 to 1536, 2048 in all
- assignment: int32 [8, 8], replicated, may hold values from 0 to 7, each once within a row
- out_weight: bfloat16 [3072, 6144], P('tensor'), may hold values from -0.109375 to 0.109375
Outputs:
- mixed: bfloat16 [2048, 6144], P(('dp', 'tensor'))
The draws below stay inside these ranges and needn't reach their ends.
Inputs may be any that keep to these rules, and one draw needn't show every extreme that they name: `lengths`: the prompts fill the 2048 positions in order, one of them exactly 1536 long. `assignment`: each row is a permutation of 0 to 7.
All inputs are finite; a program needn't handle non-finite values.
Results may differ from the reference program's by a relative error of at most 0.014.
Values may be sent and summed in bfloat16 or wider, within the bound.
A program may use at most 64 MiB of HBM per device.

```python
import math
import jax
import jax.numpy as jnp
import numpy as np
from jax import lax

D = 6144
HD = 128
HEADS = 24
KV_HEADS = 4
TOK_DEV = 256
TOKENS = 2048
PIECE = 32
MOST = 1536
DOCS = 4
N_DP = 8
N_TENSOR = 4


def paired_draw(key):
    base = jax.random.fold_in(key, 71)
    key_q, key_k = jax.random.split(base, 2)
    key_vals = jnp.clip(jax.random.normal(key_k, (TOKENS, KV_HEADS, HD), jnp.float32), -4.5, 4.5)
    query_vals = jnp.clip(jax.random.normal(key_q, (TOKENS, HEADS, HD), jnp.float32), -4.5, 4.5)
    return (query_vals.reshape(TOKENS, HEADS * HD), key_vals.reshape(TOKENS, KV_HEADS * HD))


def draw_queries(key, part):
    return paired_draw(key)[0].astype(jnp.bfloat16)


def draw_keys(key, part):
    return paired_draw(key)[1].astype(jnp.bfloat16)


def level_of(rng, dims, shards, smallest, top_value):
    loudness, own = 1.0, jax.random.fold_in(rng, 6)
    for dim, parts in shards:
        heights = jnp.exp(jax.random.uniform(jax.random.fold_in(own, dim), (parts,), jnp.float32, smallest / len(shards), top_value / len(shards)))
        loudness = loudness * jnp.repeat(heights, dims[dim] // parts).reshape([-1 if axis == dim else 1 for axis in range(len(dims))])
    return loudness


def profile(amount, total, limit, skew):
    weights = [(1 << 20) // math.isqrt(standing ** skew) + 1 for standing in range(2, amount + 1)]
    surplus, holding = total - limit - (amount - 1), [1] * (amount - 1)
    while surplus > 0:
        candidates = [i for i in range(amount - 1) if holding[i] < limit]
        pool, left = sum([weights[i] for i in candidates]), surplus
        for i in candidates:
            addition = min(limit - holding[i], max(1, left * weights[i] // pool), surplus)
            holding[i] = holding[i] + addition
            surplus = surplus - addition
    return np.array([limit] + holding)


def ragged_sizes(own_key, amount, total, reach, lean):
    if amount == 2:
        one = jax.random.randint(own_key, (), max(1, total - reach), min(reach, total - 1) + 1)
        return jnp.stack([one, total - one])
    tallies = jnp.asarray(profile(amount, total, reach, lean), jnp.int32)
    twos = (amount - 1) // 2
    giver, taker = tallies[1:1 + 2 * twos:2], tallies[2:2 + 2 * twos:2]
    room = jnp.minimum(giver - 1, reach - taker)
    moved = jax.random.randint(jax.random.fold_in(own_key, 1), (twos,), 0, 1 << 20) % (room + 1)
    tallies = tallies.at[1:1 + 2 * twos:2].set(giver - moved).at[2:2 + 2 * twos:2].set(taker + moved)
    return tallies[jax.random.permutation(jax.random.fold_in(own_key, 2), amount)]


def bell_draw(rng, dims, spread, reach, cuts=(), kind=jnp.bfloat16):
    values = jax.random.normal(rng, dims, jnp.float32) * spread
    if len(cuts) > 0:
        values = level_of(rng, dims, cuts, -0.22, 0.18) * values
    return jnp.clip(values, min=-reach, max=reach).astype(kind)


def setup_inputs(seed: int = 0) -> dict:
    key_of = jax.random.split(jax.random.key(seed), 7)
    queries = draw_queries(jax.random.fold_in(key_of[6], 71), 0)
    keys = draw_keys(jax.random.fold_in(key_of[6], 71), 0)
    values = bell_draw(key_of[2], (TOKENS, KV_HEADS * HD), 1.0, 6.0, ((0, 8),))
    lengths = ragged_sizes(key_of[3], DOCS, TOKENS, MOST, 2).astype(jnp.int32)
    assignment = jax.vmap(lambda own: jax.random.permutation(own, N_DP))(jax.random.split(key_of[4], N_DP)).reshape((N_DP, N_DP)).astype(jnp.int32)
    out_weight = bell_draw(key_of[5], (HEADS * HD, D), (HEADS * HD) ** -0.5, 0.109375, ((0, 4),))
    return {"queries": queries, "keys": keys, "values": values, "lengths": lengths, "assignment": assignment, "out_weight": out_weight}


def reference(queries, keys, values, lengths, assignment, out_weight):
    group_size = HEADS // KV_HEADS
    score_scale = HD ** -0.5
    doc_ends = jnp.cumsum(lengths).astype(jnp.int32)
    places = jnp.arange(TOKENS, dtype=jnp.int32)
    doc_all = jnp.sum((places[:, None] >= doc_ends[None, :]).astype(jnp.int32), axis=1).astype(jnp.int32)
    front_rows = MOST
    key_pad = jnp.concatenate([jnp.zeros((front_rows, KV_HEADS * HD), keys.dtype), keys], axis=0)
    value_pad = jnp.concatenate([jnp.zeros((front_rows, KV_HEADS * HD), values.dtype), values], axis=0)
    doc_pad = jnp.concatenate([jnp.full((front_rows,), -1, jnp.int32), doc_all], axis=0)
    pos_pad = jnp.arange(-front_rows, TOKENS, dtype=jnp.int32)

    def one_block(block_index):
        first_row = (block_index * TOK_DEV).astype(jnp.int32)
        query_rows = lax.dynamic_slice_in_dim(queries, first_row, TOK_DEV, 0).astype(jnp.float32)
        query_rows = query_rows.reshape(TOK_DEV, KV_HEADS, group_size, HD)
        key_rows = lax.dynamic_slice_in_dim(key_pad, first_row, front_rows + TOK_DEV, 0).astype(jnp.float32)
        key_rows = key_rows.reshape(front_rows + TOK_DEV, KV_HEADS, HD)
        value_rows = lax.dynamic_slice_in_dim(value_pad, first_row, front_rows + TOK_DEV, 0).astype(jnp.float32)
        value_rows = value_rows.reshape(front_rows + TOK_DEV, KV_HEADS, HD)
        q_pos = first_row + jnp.arange(TOK_DEV, dtype=jnp.int32)
        q_doc = lax.dynamic_slice_in_dim(doc_all, first_row, TOK_DEV, 0)
        k_pos = lax.dynamic_slice_in_dim(pos_pad, first_row, front_rows + TOK_DEV, 0)
        k_doc = lax.dynamic_slice_in_dim(doc_pad, first_row, front_rows + TOK_DEV, 0)
        visible = (k_doc[None, :] == q_doc[:, None]) & (k_pos[None, :] <= q_pos[:, None])
        scores = jnp.einsum("qcgd,kcd->cgqk", query_rows, key_rows) * score_scale
        scores = jnp.where(visible[None, None], scores, -1e30)
        highest = jnp.max(scores, axis=3)
        weights = jnp.exp(scores - highest[..., None])
        totals = jnp.sum(weights, axis=3)
        rounded = lax.optimization_barrier(weights.astype(jnp.bfloat16))
        summed = jnp.einsum("cgqk,kcd->qcgd", rounded.astype(jnp.float32), value_rows)
        result = summed / jnp.transpose(totals, (2, 0, 1))[..., None]
        return result.reshape(TOK_DEV, HEADS * HD).astype(jnp.bfloat16)

    attended = lax.map(one_block, jnp.arange(N_DP, dtype=jnp.int32))
    attended = attended.reshape(N_DP, N_DP, PIECE, HEADS * HD)
    sources = jnp.arange(N_DP, dtype=jnp.int32)
    regrouped = attended[sources[None, :], jnp.transpose(assignment)]
    regrouped = regrouped.reshape(TOKENS, HEADS * HD)
    lane_cols = HEADS * HD // N_TENSOR
    mixed = jnp.zeros((TOKENS, D), jnp.float32)
    for lane_index in range(N_TENSOR):
        term = jnp.dot(regrouped[:, lane_index * lane_cols:(lane_index + 1) * lane_cols],
                       out_weight[lane_index * lane_cols:(lane_index + 1) * lane_cols],
                       preferred_element_type=jnp.float32)
        term_b = lax.optimization_barrier(term.astype(jnp.bfloat16))
        mixed = mixed + term_b.astype(jnp.float32)
    return mixed.astype(jnp.bfloat16)
```

```python
import math

import jax
import jax.numpy as jnp
from jax import lax
from jax.experimental import pallas as pl
from jax.experimental.pallas import tpu as pltpu
from jax.sharding import PartitionSpec as P

HD = 128
HEADS = 24
KV_HEADS = 4
MESH = pl.DeviceIdType.MESH
CHUNKS = 8


def kernel(
    G, T, lengths, assignment, q_hbm, k_hbm, v_hbm, w_hbm, out_ref,
    q_all, q_stage, q_buf, k_buf, v_buf, w_buf, att, in_r, in_l, out_r, out_l,
    load_sem, w_sem, own_sem, k_send, k_recv, v_send, v_recv, q_send, q_recv,
    r_send, r_recv, l_send, l_recv,
):
    me = lax.axis_index("dp")
    z = lax.axis_index("tensor")
    tok_rows, q_width = q_all.shape
    heads_here = q_width // HD
    piece = tok_rows // G
    per_dest = G // T
    out_rows = tok_rows // T
    n_cols = w_buf.shape[1]
    cw = n_cols // CHUNKS
    kv_head = z * heads_here // (HEADS // KV_HEADS)
    kv_cols = pl.ds(pl.multiple_of(kv_head * HD, HD), HD)

    load_q = pltpu.make_async_copy(q_hbm, q_all, load_sem)
    load_q.start()
    barrier = pltpu.get_barrier_semaphore()
    for i in range(1, G):
        pl.semaphore_signal(
            barrier, inc=1, device_id=(lax.rem(me + i, G), z), device_id_type=MESH
        )
    for i in range(1, T):
        pl.semaphore_signal(
            barrier, inc=1, device_id=(me, lax.rem(z + i, T)), device_id_type=MESH
        )
    own_k = pltpu.make_async_copy(k_hbm.at[:, kv_cols], k_buf.at[me], own_sem.at[0])
    own_v = pltpu.make_async_copy(v_hbm.at[:, kv_cols], v_buf.at[me], own_sem.at[1])
    own_k.start()
    own_v.start()
    load_w = pltpu.make_async_copy(w_hbm, w_buf, w_sem)
    load_w.start()
    load_q.wait()
    place = lax.broadcasted_iota(jnp.int32, (tok_rows, 1), 0)
    source_row = jnp.zeros((tok_rows, 1), jnp.int32)
    for g in range(G):
        here = (place >= g * piece) & (place < (g + 1) * piece)
        source_row = source_row + jnp.where(here, (assignment[me, g] - g) * piece + place, 0)
    chosen = (lax.broadcasted_iota(jnp.int32, (tok_rows, tok_rows), 1) == source_row)
    picked = jnp.dot(
        chosen.astype(jnp.float32).astype(jnp.bfloat16), q_all[...],
        preferred_element_type=jnp.float32,
    ).astype(jnp.bfloat16)
    for g in range(G):
        q_stage[g] = picked[g * piece:(g + 1) * piece]
    q_buf[me] = q_stage[me]
    pl.semaphore_wait(barrier, G - 1 + T - 1)

    def q_copy(i, source):
        return pltpu.make_async_remote_copy(
            src_ref=q_stage.at[lax.rem(me + i, G)], dst_ref=q_buf.at[source],
            send_sem=q_send.at[i], recv_sem=q_recv.at[i],
            device_id=(lax.rem(me + i, G), z), device_id_type=MESH,
        )

    def k_copy(i, source):
        return pltpu.make_async_remote_copy(
            src_ref=k_hbm.at[:, kv_cols], dst_ref=k_buf.at[source],
            send_sem=k_send.at[i], recv_sem=k_recv.at[i],
            device_id=(lax.rem(me + i, G), z), device_id_type=MESH,
        )

    def v_copy(i, source):
        return pltpu.make_async_remote_copy(
            src_ref=v_hbm.at[:, kv_cols], dst_ref=v_buf.at[source],
            send_sem=v_send.at[i], recv_sem=v_recv.at[i],
            device_id=(lax.rem(me + i, G), z), device_id_type=MESH,
        )

    for copy in (q_copy, k_copy, v_copy):
        for i in range(1, G):
            copy(i, me).start()
    own_k.wait()
    own_v.wait()
    for copy in (q_copy, k_copy, v_copy):
        for i in range(1, G):
            copy(i, lax.rem(me + G - i, G)).wait_recv()

    factor = HD ** (-0.5) * math.log2(math.e)

    def attend(s):
        span = (s + 1) * tok_rows
        q_rows = q_buf[s]
        if piece % 16:
            q_rows = q_rows.astype(jnp.float32)
        rows = jnp.concatenate(
            [q_rows[:, h * HD:(h + 1) * HD] for h in range(heads_here)], axis=0
        ).astype(jnp.bfloat16)
        keys = k_buf[:s + 1].reshape(span, HD)
        vals = v_buf[:s + 1].reshape(span, HD)
        q_pos = (
            s * tok_rows + assignment[s, me] * piece
            + lax.broadcasted_iota(jnp.int32, (piece, 1), 0)
        )
        start = jnp.zeros((piece, 1), jnp.int32)
        end = jnp.int32(0)
        for n in range(lengths.shape[0]):
            end = end + lengths[n]
            start = jnp.where(q_pos >= end, end, start)
        k_pos = lax.broadcasted_iota(jnp.int32, (piece, span), 1)
        bias = jnp.where((k_pos <= q_pos) & (k_pos >= start), 0.0, -1e30)
        scores = lax.dot_general(
            rows, keys, (((1,), (1,)), ((), ())), preferred_element_type=jnp.float32
        )
        scores = scores.reshape(heads_here, piece, span) * factor + bias[None]
        highest = jnp.max(scores, axis=2, keepdims=True)
        weights = jnp.exp2(scores - highest)
        total = jnp.sum(weights, axis=2, keepdims=True)
        summed = jnp.dot(
            weights.reshape(heads_here * piece, span).astype(jnp.bfloat16), vals,
            preferred_element_type=jnp.float32,
        ).reshape(heads_here, piece, HD)
        result = (summed / total).astype(att.dtype)
        for h in range(heads_here):
            att[s * piece:(s + 1) * piece, h * HD:(h + 1) * HD] = result[h]

    def product(t, c):
        rows = att[pl.ds(pl.multiple_of(t * out_rows, out_rows), out_rows), :]
        cols = w_buf[:, pl.ds(pl.multiple_of(c * cw, cw), cw)]
        return jnp.dot(rows.astype(jnp.bfloat16), cols, preferred_element_type=jnp.float32)

    def r_copy(k):
        return pltpu.make_async_remote_copy(
            src_ref=out_r.at[k], dst_ref=in_r.at[k],
            send_sem=r_send.at[k], recv_sem=r_recv.at[k],
            device_id=(me, lax.rem(z + 1, T)), device_id_type=MESH,
        )

    def l_copy(k):
        return pltpu.make_async_remote_copy(
            src_ref=out_l.at[k], dst_ref=in_l.at[k],
            send_sem=l_send.at[k], recv_sem=l_recv.at[k],
            device_id=(me, lax.rem(z + T - 1, T)), device_id_type=MESH,
        )

    def step(k, carry):
        c = k % CHUNKS
        t_r = T - 1 - k // CHUNKS
        t_l = k // CHUNKS

        @pl.when(z < t_r)
        def _():
            out_r[k] = product(t_r, c).astype(jnp.bfloat16)

            @pl.when(z > 0)
            def _():
                r_copy(k).wait_recv()
                out_r[k] = (
                    out_r[k].astype(jnp.float32) + in_r[k].astype(jnp.float32)
                ).astype(jnp.bfloat16)

            r_copy(k).start()

        @pl.when(z > t_l)
        def _():
            out_l[k] = product(t_l, c).astype(jnp.bfloat16)

            @pl.when(z < T - 1)
            def _():
                l_copy(k).wait_recv()
                out_l[k] = (
                    out_l[k].astype(jnp.float32) + in_l[k].astype(jnp.float32)
                ).astype(jnp.bfloat16)

            l_copy(k).start()

        return carry

    early = list(range(G - per_dest, G)) + list(range(per_dest))
    for s in early:
        attend(s)
    load_w.wait()
    lax.fori_loop(0, CHUNKS, step, 0)
    for s in range(G):
        if s not in early:
            attend(s)
    lax.fori_loop(CHUNKS, (T - 1) * CHUNKS, step, 0)

    def finish(c, carry):
        cols = pl.ds(pl.multiple_of(c * cw, cw), cw)
        out_ref[:, cols] = product(z, c).astype(jnp.bfloat16)

        @pl.when(z < T - 1)
        def _():
            k = z * CHUNKS + c
            l_copy(k).wait_recv()
            out_ref[:, cols] = (
                out_ref[:, cols].astype(jnp.float32) + in_l[k].astype(jnp.float32)
            ).astype(jnp.bfloat16)

        @pl.when(z > 0)
        def _():
            k = (T - 1 - z) * CHUNKS + c
            r_copy(k).wait_recv()
            out_ref[:, cols] = (
                out_ref[:, cols].astype(jnp.float32) + in_r[k].astype(jnp.float32)
            ).astype(jnp.bfloat16)

        return carry

    lax.fori_loop(0, CHUNKS, finish, 0)

    for copy in (q_copy, k_copy, v_copy):
        for i in range(1, G):
            copy(i, me).wait_send()

    def drain(k, carry):
        @pl.when(z < T - 1 - k // CHUNKS)
        def _():
            r_copy(k).wait_send()

        @pl.when(z > k // CHUNKS)
        def _():
            l_copy(k).wait_send()

        return carry

    lax.fori_loop(0, (T - 1) * CHUNKS, drain, 0)


def local(queries, keys, values, lengths, assignment, out_weight):
    G = lax.axis_size("dp")
    T = lax.axis_size("tensor")
    tok_rows, q_width = queries.shape
    n_cols = out_weight.shape[1]
    piece = tok_rows // G
    out_rows = tok_rows // T
    cw = n_cols // CHUNKS
    slots = (T - 1) * CHUNKS
    att_type = jnp.bfloat16 if piece % 16 == 0 else jnp.float32
    smem = pl.BlockSpec(memory_space=pltpu.SMEM)
    hbm = pl.BlockSpec(memory_space=pl.ANY)
    dma = pltpu.SemaphoreType.DMA
    bf16 = jnp.bfloat16

    def body(*refs):
        kernel(G, T, *refs)

    return pl.pallas_call(
        body,
        out_shape=jax.ShapeDtypeStruct((out_rows, n_cols), bf16),
        in_specs=[smem, smem, hbm, hbm, hbm, hbm],
        out_specs=pl.BlockSpec(memory_space=pltpu.VMEM),
        scratch_shapes=[
            pltpu.VMEM((tok_rows, q_width), bf16),
            pltpu.VMEM((G, piece, q_width), bf16),
            pltpu.VMEM((G, piece, q_width), bf16),
            pltpu.VMEM((G, tok_rows, HD), bf16),
            pltpu.VMEM((G, tok_rows, HD), bf16),
            pltpu.VMEM(out_weight.shape, bf16),
            pltpu.VMEM((tok_rows, q_width), att_type),
            pltpu.VMEM((slots, out_rows, cw), bf16),
            pltpu.VMEM((slots, out_rows, cw), bf16),
            pltpu.VMEM((slots, out_rows, cw), bf16),
            pltpu.VMEM((slots, out_rows, cw), bf16),
            dma, dma, dma((2,)),
            dma((G,)), dma((G,)), dma((G,)), dma((G,)), dma((G,)), dma((G,)),
            dma((slots,)), dma((slots,)), dma((slots,)), dma((slots,)),
        ],
        compiler_params=pltpu.CompilerParams(
            collective_id=0, has_side_effects=True, vmem_limit_bytes=60 << 20
        ),
    )(lengths, assignment, queries, keys, values, out_weight)


def solution(mesh):
    in_specs = (P("dp", "tensor"), P("dp", None), P("dp", None), P(), P(), P("tensor", None))
    out_specs = P(("dp", "tensor"), None)
    return jax.shard_map(local, mesh=mesh, in_specs=in_specs, out_specs=out_specs, check_vma=False)
```

```python
import math

import jax
import jax.numpy as jnp
from jax import lax
from jax.experimental import pallas as pl
from jax.experimental.pallas import tpu as pltpu
from jax.sharding import PartitionSpec as P

HD = 128
HEADS = 24
KV_HEADS = 4
MESH = pl.DeviceIdType.MESH
CHUNKS = 8


def kernel(
    G, T, lengths, assignment, q_hbm, k_hbm, v_hbm, w_hbm, out_ref,
    q_all, q_stage, q_buf, k_buf, v_buf, w_buf, att, in_r, in_l, out_r, out_l,
    load_sem, w_sem, own_sem, k_send, k_recv, v_send, v_recv, q_send, q_recv,
    r_send, r_recv, l_send, l_recv,
):
    me = lax.axis_index("dp")
    z = lax.axis_index("tensor")
    tok_rows, q_width = q_all.shape
    heads_here = q_width // HD
    piece = tok_rows // G
    per_dest = G // T
    out_rows = tok_rows // T
    n_cols = w_buf.shape[1]
    cw = n_cols // CHUNKS
    kv_head = z * heads_here // (HEADS // KV_HEADS)
    kv_cols = pl.ds(pl.multiple_of(kv_head * HD, HD), HD)

    load_q = pltpu.make_async_copy(q_hbm, q_all, load_sem)
    load_q.start()
    barrier = pltpu.get_barrier_semaphore()
    for i in range(1, G):
        pl.semaphore_signal(
            barrier, inc=1, device_id=(lax.rem(me + i, G), z), device_id_type=MESH
        )
    for i in range(1, T):
        pl.semaphore_signal(
            barrier, inc=1, device_id=(me, lax.rem(z + i, T)), device_id_type=MESH
        )
    own_k = pltpu.make_async_copy(k_hbm.at[:, kv_cols], k_buf.at[me], own_sem.at[0])
    own_v = pltpu.make_async_copy(v_hbm.at[:, kv_cols], v_buf.at[me], own_sem.at[1])
    own_k.start()
    own_v.start()
    load_w = pltpu.make_async_copy(w_hbm, w_buf, w_sem)
    load_w.start()
    load_q.wait()
    place = lax.broadcasted_iota(jnp.int32, (tok_rows, 1), 0)
    source_row = jnp.zeros((tok_rows, 1), jnp.int32)
    for g in range(G):
        here = (place >= g * piece) & (place < (g + 1) * piece)
        source_row = source_row + jnp.where(here, (assignment[me, g] - g) * piece + place, 0)
    chosen = (lax.broadcasted_iota(jnp.int32, (tok_rows, tok_rows), 1) == source_row)
    picked = jnp.dot(
        chosen.astype(jnp.float32).astype(jnp.bfloat16), q_all[...],
        preferred_element_type=jnp.float32,
    ).astype(jnp.bfloat16)
    for g in range(G):
        q_stage[g] = picked[g * piece:(g + 1) * piece]
    q_buf[me] = q_stage[me]
    pl.semaphore_wait(barrier, G - 1 + T - 1)

    def q_copy(i, source):
        return pltpu.make_async_remote_copy(
            src_ref=q_stage.at[lax.rem(me + i, G)], dst_ref=q_buf.at[source],
            send_sem=q_send.at[i], recv_sem=q_recv.at[i],
            device_id=(lax.rem(me + i, G), z), device_id_type=MESH,
        )

    def k_copy(i, source):
        return pltpu.make_async_remote_copy(
            src_ref=k_hbm.at[:, kv_cols], dst_ref=k_buf.at[source],
            send_sem=k_send.at[i], recv_sem=k_recv.at[i],
            device_id=(lax.rem(me + i, G), z), device_id_type=MESH,
        )

    def v_copy(i, source):
        return pltpu.make_async_remote_copy(
            src_ref=v_hbm.at[:, kv_cols], dst_ref=v_buf.at[source],
            send_sem=v_send.at[i], recv_sem=v_recv.at[i],
            device_id=(lax.rem(me + i, G), z), device_id_type=MESH,
        )

    for copy in (q_copy, k_copy, v_copy):
        for i in range(1, G):
            copy(i, me).start()
    own_k.wait()
    own_v.wait()
    for copy in (q_copy, k_copy, v_copy):
        for i in range(1, G):
            copy(i, lax.rem(me + G - i, G)).wait_recv()

    factor = HD ** (-0.5) * math.log2(math.e)

    def attend(s):
        span = (s + 1) * tok_rows
        q_rows = q_buf[s]
        if piece % 16:
            q_rows = q_rows.astype(jnp.float32)
        rows = jnp.concatenate(
            [q_rows[:, h * HD:(h + 1) * HD] for h in range(heads_here)], axis=0
        ).astype(jnp.bfloat16)
        keys = k_buf[:s + 1].reshape(span, HD)
        vals = v_buf[:s + 1].reshape(span, HD)
        q_pos = (
            s * tok_rows + assignment[s, me] * piece
            + lax.broadcasted_iota(jnp.int32, (piece, 1), 0)
        )
        start = jnp.zeros((piece, 1), jnp.int32)
        end = jnp.int32(0)
        for n in range(lengths.shape[0]):
            end = end + lengths[n]
            start = jnp.where(q_pos >= end, end, start)
        k_pos = lax.broadcasted_iota(jnp.int32, (piece, span), 1)
        bias = jnp.where((k_pos <= q_pos) & (k_pos >= start), 0.0, -1e30)
        scores = lax.dot_general(
            rows, keys, (((1,), (1,)), ((), ())), preferred_element_type=jnp.float32
        )
        scores = scores.reshape(heads_here, piece, span) * factor + bias[None]
        highest = jnp.max(scores, axis=2, keepdims=True)
        weights = jnp.exp2(scores - highest)
        total = jnp.sum(weights, axis=2, keepdims=True)
        summed = jnp.dot(
            weights.reshape(heads_here * piece, span).astype(jnp.bfloat16), vals,
            preferred_element_type=jnp.float32,
        ).reshape(heads_here, piece, HD)
        result = (summed / total).astype(att.dtype)
        for h in range(heads_here):
            att[s * piece:(s + 1) * piece, h * HD:(h + 1) * HD] = result[h]

    def product(t, c):
        rows = att[pl.ds(pl.multiple_of(t * out_rows, out_rows), out_rows), :]
        cols = w_buf[:, pl.ds(pl.multiple_of(c * cw, cw), cw)]
        return jnp.dot(rows.astype(jnp.bfloat16), cols, preferred_element_type=jnp.float32)

    def r_copy(k):
        return pltpu.make_async_remote_copy(
            src_ref=out_r.at[k], dst_ref=in_r.at[k],
            send_sem=r_send.at[k], recv_sem=r_recv.at[k],
            device_id=(me, lax.rem(z + 1, T)), device_id_type=MESH,
        )

    def l_copy(k):
        return pltpu.make_async_remote_copy(
            src_ref=out_l.at[k], dst_ref=in_l.at[k],
            send_sem=l_send.at[k], recv_sem=l_recv.at[k],
            device_id=(me, lax.rem(z + T - 1, T)), device_id_type=MESH,
        )

    def right(k):
        c = k % CHUNKS
        t = T - 1 - k // CHUNKS

        @pl.when(z < t)
        def _():
            out_r[k] = product(t, c).astype(jnp.bfloat16)

            @pl.when(z > 0)
            def _():
                r_copy(k).wait_recv()
                out_r[k] = (
                    out_r[k].astype(jnp.float32) + in_r[k].astype(jnp.float32)
                ).astype(jnp.bfloat16)

            r_copy(k).start()

    def left(k):
        c = k % CHUNKS
        t = k // CHUNKS

        @pl.when(z > t)
        def _():
            out_l[k] = product(t, c).astype(jnp.bfloat16)

            @pl.when(z < T - 1)
            def _():
                l_copy(k).wait_recv()
                out_l[k] = (
                    out_l[k].astype(jnp.float32) + in_l[k].astype(jnp.float32)
                ).astype(jnp.bfloat16)

            l_copy(k).start()

    def step(k, carry):
        @pl.when(z < T // 2)
        def _():
            right(k)
            left(k)

        @pl.when(z >= T // 2)
        def _():
            left(k)
            right(k)

        return carry

    early = list(range(G - per_dest, G)) + list(range(per_dest))
    for s in early:
        attend(s)
    load_w.wait()
    lax.fori_loop(0, CHUNKS, step, 0)
    for s in range(G):
        if s not in early:
            attend(s)
    lax.fori_loop(CHUNKS, (T - 1) * CHUNKS, step, 0)

    def finish(c, carry):
        cols = pl.ds(pl.multiple_of(c * cw, cw), cw)
        out_ref[:, cols] = product(z, c).astype(jnp.bfloat16)

        @pl.when(z < T - 1)
        def _():
            k = z * CHUNKS + c
            l_copy(k).wait_recv()
            out_ref[:, cols] = (
                out_ref[:, cols].astype(jnp.float32) + in_l[k].astype(jnp.float32)
            ).astype(jnp.bfloat16)

        @pl.when(z > 0)
        def _():
            k = (T - 1 - z) * CHUNKS + c
            r_copy(k).wait_recv()
            out_ref[:, cols] = (
                out_ref[:, cols].astype(jnp.float32) + in_r[k].astype(jnp.float32)
            ).astype(jnp.bfloat16)

        return carry

    lax.fori_loop(0, CHUNKS, finish, 0)

    for copy in (q_copy, k_copy, v_copy):
        for i in range(1, G):
            copy(i, me).wait_send()

    def drain(k, carry):
        @pl.when(z < T - 1 - k // CHUNKS)
        def _():
            r_copy(k).wait_send()

        @pl.when(z > k // CHUNKS)
        def _():
            l_copy(k).wait_send()

        return carry

    lax.fori_loop(0, (T - 1) * CHUNKS, drain, 0)


def local(queries, keys, values, lengths, assignment, out_weight):
    G = lax.axis_size("dp")
    T = lax.axis_size("tensor")
    tok_rows, q_width = queries.shape
    n_cols = out_weight.shape[1]
    piece = tok_rows // G
    out_rows = tok_rows // T
    cw = n_cols // CHUNKS
    slots = (T - 1) * CHUNKS
    att_type = jnp.bfloat16 if piece % 16 == 0 else jnp.float32
    smem = pl.BlockSpec(memory_space=pltpu.SMEM)
    hbm = pl.BlockSpec(memory_space=pl.ANY)
    dma = pltpu.SemaphoreType.DMA
    bf16 = jnp.bfloat16

    def body(*refs):
        kernel(G, T, *refs)

    return pl.pallas_call(
        body,
        out_shape=jax.ShapeDtypeStruct((out_rows, n_cols), bf16),
        in_specs=[smem, smem, hbm, hbm, hbm, hbm],
        out_specs=pl.BlockSpec(memory_space=pltpu.VMEM),
        scratch_shapes=[
            pltpu.VMEM((tok_rows, q_width), bf16),
            pltpu.VMEM((G, piece, q_width), bf16),
            pltpu.VMEM((G, piece, q_width), bf16),
            pltpu.VMEM((G, tok_rows, HD), bf16),
            pltpu.VMEM((G, tok_rows, HD), bf16),
            pltpu.VMEM(out_weight.shape, bf16),
            pltpu.VMEM((tok_rows, q_width), att_type),
            pltpu.VMEM((slots, out_rows, cw), bf16),
            pltpu.VMEM((slots, out_rows, cw), bf16),
            pltpu.VMEM((slots, out_rows, cw), bf16),
            pltpu.VMEM((slots, out_rows, cw), bf16),
            dma, dma, dma((2,)),
            dma((G,)), dma((G,)), dma((G,)), dma((G,)), dma((G,)), dma((G,)),
            dma((slots,)), dma((slots,)), dma((slots,)), dma((slots,)),
        ],
        compiler_params=pltpu.CompilerParams(
            collective_id=0, has_side_effects=True, vmem_limit_bytes=60 << 20
        ),
    )(lengths, assignment, queries, keys, values, out_weight)


def solution(mesh):
    in_specs = (P("dp", "tensor"), P("dp", None), P("dp", None), P(), P(), P("tensor", None))
    out_specs = P(("dp", "tensor"), None)
    return jax.shard_map(local, mesh=mesh, in_specs=in_specs, out_specs=out_specs, check_vma=False)
```

```python
import math

import jax
import jax.numpy as jnp
from jax import lax
from jax.experimental import pallas as pl
from jax.experimental.pallas import tpu as pltpu
from jax.sharding import PartitionSpec as P

HD = 128
HEADS = 24
KV_HEADS = 4
MESH = pl.DeviceIdType.MESH
CHUNKS = 8


def kernel(
    G, T, lengths, assignment, q_hbm, k_hbm, v_hbm, w_hbm, out_ref,
    q_all, q_stage, q_buf, k_buf, v_buf, w_buf, att, in_r, in_l, out_r, out_l,
    load_sem, w_sem, own_sem, k_send, k_recv, v_send, v_recv, q_send, q_recv,
    r_send, r_recv, l_send, l_recv,
    w_far, att_far, far_send, far_recv, near_send, near_recv, row_send, row_recv,
):
    me = lax.axis_index("dp")
    z = lax.axis_index("tensor")
    tok_rows, q_width = q_all.shape
    heads_here = q_width // HD
    piece = tok_rows // G
    per_dest = G // T
    out_rows = tok_rows // T
    n_cols = w_buf.shape[1]
    cw = n_cols // CHUNKS
    early_chunks = CHUNKS // 2
    half = (T - 1) * early_chunks
    parts, far_rows, far_cols = w_far.shape
    share_rows = far_rows * parts // G
    low, high = z == 0, z == T - 1
    next_low, next_high = z == 1, z == T - 2
    partner = me + 1 - 2 * (me % 2)
    kv_head = z * heads_here // (HEADS // KV_HEADS)
    kv_cols = pl.ds(pl.multiple_of(kv_head * HD, HD), HD)

    load_q = pltpu.make_async_copy(q_hbm, q_all, load_sem)
    load_q.start()
    barrier = pltpu.get_barrier_semaphore()
    for i in range(1, G):
        pl.semaphore_signal(
            barrier, inc=1, device_id=(lax.rem(me + i, G), z), device_id_type=MESH
        )
    for i in range(1, T):
        pl.semaphore_signal(
            barrier, inc=1, device_id=(me, lax.rem(z + i, T)), device_id_type=MESH
        )
    own_k = pltpu.make_async_copy(k_hbm.at[:, kv_cols], k_buf.at[me], own_sem.at[0])
    own_v = pltpu.make_async_copy(v_hbm.at[:, kv_cols], v_buf.at[me], own_sem.at[1])
    own_k.start()
    own_v.start()
    load_w = pltpu.make_async_copy(w_hbm, w_buf, w_sem)
    load_w.start()
    load_q.wait()
    place = lax.broadcasted_iota(jnp.int32, (tok_rows, 1), 0)
    source_row = jnp.zeros((tok_rows, 1), jnp.int32)
    for g in range(G):
        here = (place >= g * piece) & (place < (g + 1) * piece)
        source_row = source_row + jnp.where(here, (assignment[me, g] - g) * piece + place, 0)
    chosen = (lax.broadcasted_iota(jnp.int32, (tok_rows, tok_rows), 1) == source_row)
    picked = jnp.dot(
        chosen.astype(jnp.float32).astype(jnp.bfloat16), q_all[...],
        preferred_element_type=jnp.float32,
    ).astype(jnp.bfloat16)
    for g in range(G):
        q_stage[g] = picked[g * piece:(g + 1) * piece]
    q_buf[me] = q_stage[me]
    pl.semaphore_wait(barrier, G - 1 + T - 1)

    def q_copy(i, source):
        return pltpu.make_async_remote_copy(
            src_ref=q_stage.at[lax.rem(me + i, G)], dst_ref=q_buf.at[source],
            send_sem=q_send.at[i], recv_sem=q_recv.at[i],
            device_id=(lax.rem(me + i, G), z), device_id_type=MESH,
        )

    def k_copy(i, source):
        return pltpu.make_async_remote_copy(
            src_ref=k_hbm.at[:, kv_cols], dst_ref=k_buf.at[source],
            send_sem=k_send.at[i], recv_sem=k_recv.at[i],
            device_id=(lax.rem(me + i, G), z), device_id_type=MESH,
        )

    def v_copy(i, source):
        return pltpu.make_async_remote_copy(
            src_ref=v_hbm.at[:, kv_cols], dst_ref=v_buf.at[source],
            send_sem=v_send.at[i], recv_sem=v_recv.at[i],
            device_id=(lax.rem(me + i, G), z), device_id_type=MESH,
        )

    def share(j):
        rows = pl.ds(pl.multiple_of((j // parts) * share_rows, share_rows), share_rows)
        return w_far.at[j % parts, rows, :]

    def far_copy():
        rows = pl.ds(pl.multiple_of((me // parts) * share_rows, share_rows), share_rows)
        first = early_chunks * cw + (me % parts) * far_cols
        cols = pl.ds(pl.multiple_of(first, far_cols), far_cols)
        return pltpu.make_async_remote_copy(
            src_ref=w_hbm.at[rows, cols], dst_ref=share(me),
            send_sem=far_send, recv_sem=far_recv,
            device_id=(me, jnp.where(z == 0, 1, T - 2)), device_id_type=MESH,
        )

    def peer_copy(i, owner):
        return pltpu.make_async_remote_copy(
            src_ref=share(owner), dst_ref=share(owner),
            send_sem=near_send.at[i], recv_sem=near_recv.at[i],
            device_id=(lax.rem(me + 2 * i, G), z), device_id_type=MESH,
        )

    def pass_copy(i, owner):
        return pltpu.make_async_remote_copy(
            src_ref=share(owner), dst_ref=share(owner),
            send_sem=near_send.at[G // 2 + i], recv_sem=near_recv.at[G // 2 + i],
            device_id=(partner, z), device_id_type=MESH,
        )

    def row_copy(t):
        rows = pl.ds(t * out_rows, out_rows)
        return pltpu.make_async_remote_copy(
            src_ref=att.at[rows, :], dst_ref=att_far.at[rows, :],
            send_sem=row_send.at[t], recv_sem=row_recv.at[t],
            device_id=(me, jnp.where(z == 0, 1, T - 2)), device_id_type=MESH,
        )

    @pl.when(low | high)
    def _():
        far_copy().start()

    for copy in (q_copy, k_copy, v_copy):
        for i in range(1, G):
            copy(i, me).start()
    own_k.wait()
    own_v.wait()
    for copy in (q_copy, k_copy, v_copy):
        for i in range(1, G):
            copy(i, lax.rem(me + G - i, G)).wait_recv()

    @pl.when(next_low | next_high)
    def _():
        far_copy().wait_recv()
        for i in range(1, G // 2):
            peer_copy(i, me).start()
        pass_copy(0, me).start()

    factor = HD ** (-0.5) * math.log2(math.e)

    def attend(s):
        span = (s + 1) * tok_rows
        q_rows = q_buf[s]
        if piece % 16:
            q_rows = q_rows.astype(jnp.float32)
        rows = jnp.concatenate(
            [q_rows[:, h * HD:(h + 1) * HD] for h in range(heads_here)], axis=0
        ).astype(jnp.bfloat16)
        keys = k_buf[:s + 1].reshape(span, HD)
        vals = v_buf[:s + 1].reshape(span, HD)
        q_pos = (
            s * tok_rows + assignment[s, me] * piece
            + lax.broadcasted_iota(jnp.int32, (piece, 1), 0)
        )
        start = jnp.zeros((piece, 1), jnp.int32)
        end = jnp.int32(0)
        for n in range(lengths.shape[0]):
            end = end + lengths[n]
            start = jnp.where(q_pos >= end, end, start)
        k_pos = lax.broadcasted_iota(jnp.int32, (piece, span), 1)
        bias = jnp.where((k_pos <= q_pos) & (k_pos >= start), 0.0, -1e30)
        scores = lax.dot_general(
            rows, keys, (((1,), (1,)), ((), ())), preferred_element_type=jnp.float32
        )
        scores = scores.reshape(heads_here, piece, span) * factor + bias[None]
        highest = jnp.max(scores, axis=2, keepdims=True)
        weights = jnp.exp2(scores - highest)
        total = jnp.sum(weights, axis=2, keepdims=True)
        summed = jnp.dot(
            weights.reshape(heads_here * piece, span).astype(jnp.bfloat16), vals,
            preferred_element_type=jnp.float32,
        ).reshape(heads_here, piece, HD)
        result = (summed / total).astype(att.dtype)
        for h in range(heads_here):
            att[s * piece:(s + 1) * piece, h * HD:(h + 1) * HD] = result[h]

    def product(t, c):
        rows = att[pl.ds(pl.multiple_of(t * out_rows, out_rows), out_rows), :]
        cols = w_buf[:, pl.ds(pl.multiple_of(c * cw, cw), cw)]
        return jnp.dot(rows.astype(jnp.bfloat16), cols, preferred_element_type=jnp.float32)

    def r_copy(k):
        return pltpu.make_async_remote_copy(
            src_ref=out_r.at[k], dst_ref=in_r.at[k],
            send_sem=r_send.at[k], recv_sem=r_recv.at[k],
            device_id=(me, lax.rem(z + 1, T)), device_id_type=MESH,
        )

    def l_copy(k):
        return pltpu.make_async_remote_copy(
            src_ref=out_l.at[k], dst_ref=in_l.at[k],
            send_sem=l_send.at[k], recv_sem=l_recv.at[k],
            device_id=(me, lax.rem(z + T - 1, T)), device_id_type=MESH,
        )

    def far_product(t, c):
        rows = att_far[pl.ds(pl.multiple_of(t * out_rows, out_rows), out_rows), :]
        rows = rows.astype(jnp.bfloat16)
        per_chunk = cw // far_cols
        return jnp.concatenate(
            [
                jnp.dot(
                    rows, w_far[(c - early_chunks) * per_chunk + n],
                    preferred_element_type=jnp.float32,
                )
                for n in range(per_chunk)
            ],
            axis=1,
        )

    def add_to(ref, index, more):
        ref[index] = (ref[index].astype(jnp.float32) + more).astype(jnp.bfloat16)

    def place_of(k):
        return k % half // early_chunks, k // half * early_chunks + k % early_chunks

    def right(k):
        n, c = place_of(k)
        t = T - 1 - n
        late = k >= half

        @pl.when((z < t) & ((z > 0) | (k < half)))
        def _():
            out_r[k] = product(t, c).astype(jnp.bfloat16)

            @pl.when((z > 1) | ((z == 1) & (k < half)))
            def _():
                r_copy(k).wait_recv()
                add_to(out_r, k, in_r[k].astype(jnp.float32))

            @pl.when((z == 1) & late)
            def _():
                add_to(out_r, k, far_product(t, c))

            r_copy(k).start()

    def left(k):
        t, c = place_of(k)
        late = k >= half

        @pl.when((z > t) & ((z < T - 1) | (k < half)))
        def _():
            out_l[k] = product(t, c).astype(jnp.bfloat16)

            @pl.when((z < T - 2) | ((z == T - 2) & (k < half)))
            def _():
                l_copy(k).wait_recv()
                add_to(out_l, k, in_l[k].astype(jnp.float32))

            @pl.when((z == T - 2) & late)
            def _():
                add_to(out_l, k, far_product(t, c))

            l_copy(k).start()

    def step(k, carry):
        @pl.when(z < T // 2)
        def _():
            right(k)
            left(k)

        @pl.when(z >= T // 2)
        def _():
            left(k)
            right(k)

        return carry

    def send_rows(t):
        @pl.when((low & (t > 0)) | (high & (t < T - 1)))
        def _():
            row_copy(t).start()

    early = (T - 1, 0)
    for t in early:
        for s in range(t * per_dest, (t + 1) * per_dest):
            attend(s)
    load_w.wait()
    lax.fori_loop(0, early_chunks, step, 0)
    for t in range(T):
        if t not in early:
            for s in range(t * per_dest, (t + 1) * per_dest):
                attend(s)

    @pl.when(next_low | next_high)
    def _():
        for i in range(1, G // 2):
            owner = lax.rem(me + G - 2 * i, G)
            peer_copy(i, owner).wait_recv()
            pass_copy(i, owner).start()

    for t in range(T):
        send_rows(t)
    lax.fori_loop(early_chunks, half, step, 0)

    @pl.when(next_low | next_high)
    def _():
        for i in range(G // 2):
            pass_copy(i, lax.rem(partner + G - 2 * i, G)).wait_recv()
        for t in range(T):
            @pl.when((next_low & (t > 0)) | (next_high & (t < T - 1)))
            def _():
                row_copy(t).wait_recv()

    lax.fori_loop(half, 2 * half, step, 0)

    def finish(c, carry):
        cols = pl.ds(pl.multiple_of(c * cw, cw), cw)
        late = c >= early_chunks
        base = c // early_chunks * half + c % early_chunks

        def add_out(more):
            out_ref[:, cols] = (out_ref[:, cols].astype(jnp.float32) + more).astype(jnp.bfloat16)

        out_ref[:, cols] = product(z, c).astype(jnp.bfloat16)

        @pl.when((next_low | next_high) & late)
        def _():
            add_out(far_product(z, c))

        @pl.when((z < T - 2) | ((z == T - 2) & (c < early_chunks)))
        def _():
            k = base + z * early_chunks
            l_copy(k).wait_recv()
            add_out(in_l[k].astype(jnp.float32))

        @pl.when((z > 1) | ((z == 1) & (c < early_chunks)))
        def _():
            k = base + (T - 1 - z) * early_chunks
            r_copy(k).wait_recv()
            add_out(in_r[k].astype(jnp.float32))

        return carry

    lax.fori_loop(0, CHUNKS, finish, 0)

    for copy in (q_copy, k_copy, v_copy):
        for i in range(1, G):
            copy(i, me).wait_send()

    @pl.when(low | high)
    def _():
        far_copy().wait_send()
        for t in range(T):
            @pl.when((low & (t > 0)) | (high & (t < T - 1)))
            def _():
                row_copy(t).wait_send()

    @pl.when(next_low | next_high)
    def _():
        for i in range(1, G // 2):
            peer_copy(i, me).wait_send()
        for i in range(G // 2):
            pass_copy(i, lax.rem(me + G - 2 * i, G)).wait_send()

    def drain(k, carry):
        n, _ = place_of(k)

        @pl.when((z < T - 1 - n) & ((z > 0) | (k < half)))
        def _():
            r_copy(k).wait_send()

        @pl.when((z > n) & ((z < T - 1) | (k < half)))
        def _():
            l_copy(k).wait_send()

        return carry

    lax.fori_loop(0, 2 * half, drain, 0)


def local(queries, keys, values, lengths, assignment, out_weight):
    G = lax.axis_size("dp")
    T = lax.axis_size("tensor")
    tok_rows, q_width = queries.shape
    n_cols = out_weight.shape[1]
    piece = tok_rows // G
    out_rows = tok_rows // T
    cw = n_cols // CHUNKS
    slots = (T - 1) * CHUNKS
    parts = CHUNKS
    far_cols = CHUNKS // 2 * cw // parts
    att_type = jnp.bfloat16 if piece % 16 == 0 else jnp.float32
    smem = pl.BlockSpec(memory_space=pltpu.SMEM)
    hbm = pl.BlockSpec(memory_space=pl.ANY)
    dma = pltpu.SemaphoreType.DMA
    bf16 = jnp.bfloat16

    def body(*refs):
        kernel(G, T, *refs)

    return pl.pallas_call(
        body,
        out_shape=jax.ShapeDtypeStruct((out_rows, n_cols), bf16),
        in_specs=[smem, smem, hbm, hbm, hbm, hbm],
        out_specs=pl.BlockSpec(memory_space=pltpu.VMEM),
        scratch_shapes=[
            pltpu.VMEM((tok_rows, q_width), bf16),
            pltpu.VMEM((G, piece, q_width), bf16),
            pltpu.VMEM((G, piece, q_width), bf16),
            pltpu.VMEM((G, tok_rows, HD), bf16),
            pltpu.VMEM((G, tok_rows, HD), bf16),
            pltpu.VMEM(out_weight.shape, bf16),
            pltpu.VMEM((tok_rows, q_width), att_type),
            pltpu.VMEM((slots, out_rows, cw), bf16),
            pltpu.VMEM((slots, out_rows, cw), bf16),
            pltpu.VMEM((slots, out_rows, cw), bf16),
            pltpu.VMEM((slots, out_rows, cw), bf16),
            dma, dma, dma((2,)),
            dma((G,)), dma((G,)), dma((G,)), dma((G,)), dma((G,)), dma((G,)),
            dma((slots,)), dma((slots,)), dma((slots,)), dma((slots,)),
            pltpu.VMEM((parts, q_width, far_cols), bf16),
            pltpu.VMEM((tok_rows, q_width), att_type),
            dma, dma, dma((G,)), dma((G,)), dma((T,)), dma((T,)),
        ],
        compiler_params=pltpu.CompilerParams(
            collective_id=0, has_side_effects=True, vmem_limit_bytes=60 << 20
        ),
    )(lengths, assignment, queries, keys, values, out_weight)


def solution(mesh):
    in_specs = (P("dp", "tensor"), P("dp", None), P("dp", None), P(), P(), P("tensor", None))
    out_specs = P(("dp", "tensor"), None)
    return jax.shard_map(local, mesh=mesh, in_specs=in_specs, out_specs=out_specs, check_vma=False)
```

```python
import math

import jax
import jax.numpy as jnp
from jax import lax
from jax.experimental import pallas as pl
from jax.experimental.pallas import tpu as pltpu
from jax.sharding import PartitionSpec as P

HD = 128
HEADS = 24
KV_HEADS = 4
MESH = pl.DeviceIdType.MESH
CHUNKS = 8
LAG = 3


def kernel(
    G, T, lengths, assignment, q_hbm, k_hbm, v_hbm, w_hbm, out_ref,
    q_all, q_stage, q_buf, k_buf, v_buf, w_buf, att, in_r, in_l, out_r, out_l,
    load_sem, w_sem, own_sem, k_send, k_recv, v_send, v_recv, q_send, q_recv,
    r_send, r_recv, l_send, l_recv,
    w_far, att_far, far_send, far_recv, near_send, near_recv, row_send, row_recv,
):
    me = lax.axis_index("dp")
    z = lax.axis_index("tensor")
    tok_rows, q_width = q_all.shape
    heads_here = q_width // HD
    piece = tok_rows // G
    per_dest = G // T
    out_rows = tok_rows // T
    n_cols = w_buf.shape[1]
    cw = n_cols // CHUNKS
    early_chunks = CHUNKS // 2
    half = (T - 1) * early_chunks
    parts, far_rows, far_cols = w_far.shape
    share_rows = far_rows * parts // G
    low, high = z == 0, z == T - 1
    next_low, next_high = z == 1, z == T - 2
    partner = me + 1 - 2 * (me % 2)
    kv_head = z * heads_here // (HEADS // KV_HEADS)
    kv_cols = pl.ds(pl.multiple_of(kv_head * HD, HD), HD)

    load_q = pltpu.make_async_copy(q_hbm, q_all, load_sem)
    load_q.start()
    barrier = pltpu.get_barrier_semaphore()
    for i in range(1, G):
        pl.semaphore_signal(
            barrier, inc=1, device_id=(lax.rem(me + i, G), z), device_id_type=MESH
        )
    for i in range(1, T):
        pl.semaphore_signal(
            barrier, inc=1, device_id=(me, lax.rem(z + i, T)), device_id_type=MESH
        )
    own_k = pltpu.make_async_copy(k_hbm.at[:, kv_cols], k_buf.at[me], own_sem.at[0])
    own_v = pltpu.make_async_copy(v_hbm.at[:, kv_cols], v_buf.at[me], own_sem.at[1])
    own_k.start()
    own_v.start()
    load_w = pltpu.make_async_copy(w_hbm, w_buf, w_sem)
    load_w.start()
    load_q.wait()
    place = lax.broadcasted_iota(jnp.int32, (tok_rows, 1), 0)
    source_row = jnp.zeros((tok_rows, 1), jnp.int32)
    for g in range(G):
        here = (place >= g * piece) & (place < (g + 1) * piece)
        source_row = source_row + jnp.where(here, (assignment[me, g] - g) * piece + place, 0)
    chosen = (lax.broadcasted_iota(jnp.int32, (tok_rows, tok_rows), 1) == source_row)
    picked = jnp.dot(
        chosen.astype(jnp.float32).astype(jnp.bfloat16), q_all[...],
        preferred_element_type=jnp.float32,
    ).astype(jnp.bfloat16)
    for g in range(G):
        q_stage[g] = picked[g * piece:(g + 1) * piece]
    q_buf[me] = q_stage[me]
    pl.semaphore_wait(barrier, G - 1 + T - 1)

    def q_copy(i, source):
        return pltpu.make_async_remote_copy(
            src_ref=q_stage.at[lax.rem(me + i, G)], dst_ref=q_buf.at[source],
            send_sem=q_send.at[i], recv_sem=q_recv.at[i],
            device_id=(lax.rem(me + i, G), z), device_id_type=MESH,
        )

    def once_copy(which, i, source):
        hbm, buf, send, recv = which
        return pltpu.make_async_remote_copy(
            src_ref=hbm.at[:, kv_cols], dst_ref=buf.at[source],
            send_sem=send.at[i], recv_sem=recv.at[i],
            device_id=(lax.rem(me + 2 * i, G), z), device_id_type=MESH,
        )

    def partner_copy(which, i, source):
        hbm, buf, send, recv = which
        return pltpu.make_async_remote_copy(
            src_ref=hbm.at[:, kv_cols] if i == 0 else buf.at[source], dst_ref=buf.at[source],
            send_sem=send.at[G // 2 + i], recv_sem=recv.at[G // 2 + i],
            device_id=(partner, z), device_id_type=MESH,
        )

    both = ((k_hbm, k_buf, k_send, k_recv), (v_hbm, v_buf, v_send, v_recv))

    def share(j):
        rows = pl.ds(pl.multiple_of((j // parts) * share_rows, share_rows), share_rows)
        return w_far.at[j % parts, rows, :]

    def far_copy():
        rows = pl.ds(pl.multiple_of((me // parts) * share_rows, share_rows), share_rows)
        first = early_chunks * cw + (me % parts) * far_cols
        cols = pl.ds(pl.multiple_of(first, far_cols), far_cols)
        return pltpu.make_async_remote_copy(
            src_ref=w_hbm.at[rows, cols], dst_ref=share(me),
            send_sem=far_send, recv_sem=far_recv,
            device_id=(me, jnp.where(z == 0, 1, T - 2)), device_id_type=MESH,
        )

    def peer_copy(i, owner):
        return pltpu.make_async_remote_copy(
            src_ref=share(owner), dst_ref=share(owner),
            send_sem=near_send.at[i], recv_sem=near_recv.at[i],
            device_id=(lax.rem(me + 2 * i, G), z), device_id_type=MESH,
        )

    def pass_copy(i, owner):
        return pltpu.make_async_remote_copy(
            src_ref=share(owner), dst_ref=share(owner),
            send_sem=near_send.at[G // 2 + i], recv_sem=near_recv.at[G // 2 + i],
            device_id=(partner, z), device_id_type=MESH,
        )

    def row_copy(t):
        rows = pl.ds(t * out_rows, out_rows)
        return pltpu.make_async_remote_copy(
            src_ref=att.at[rows, :], dst_ref=att_far.at[rows, :],
            send_sem=row_send.at[t], recv_sem=row_recv.at[t],
            device_id=(me, jnp.where(z == 0, 1, T - 2)), device_id_type=MESH,
        )

    @pl.when(low | high)
    def _():
        far_copy().start()

    for which in both:
        for i in range(1, G // 2):
            once_copy(which, i, me).start()
    for which in both:
        partner_copy(which, 0, me).start()
    for i in range(1, G):
        q_copy(i, me).start()
    own_k.wait()
    own_v.wait()
    for which in both:
        for i in range(1, G // 2):
            source = lax.rem(me + G - 2 * i, G)
            once_copy(which, i, source).wait_recv()
            partner_copy(which, i, source).start()
    for which in both:
        for i in range(G // 2):
            partner_copy(which, i, lax.rem(partner + G - 2 * i, G)).wait_recv()
    for i in range(1, G):
        q_copy(i, lax.rem(me + G - i, G)).wait_recv()

    @pl.when(next_low | next_high)
    def _():
        far_copy().wait_recv()
        for i in range(1, G // 2):
            peer_copy(i, me).start()
        pass_copy(0, me).start()

    factor = HD ** (-0.5) * math.log2(math.e)

    def attend(s):
        span = (s + 1) * tok_rows
        q_rows = q_buf[s]
        if piece % 16:
            q_rows = q_rows.astype(jnp.float32)
        rows = jnp.concatenate(
            [q_rows[:, h * HD:(h + 1) * HD] for h in range(heads_here)], axis=0
        ).astype(jnp.bfloat16)
        keys = k_buf[:s + 1].reshape(span, HD)
        vals = v_buf[:s + 1].reshape(span, HD)
        q_pos = (
            s * tok_rows + assignment[s, me] * piece
            + lax.broadcasted_iota(jnp.int32, (piece, 1), 0)
        )
        start = jnp.zeros((piece, 1), jnp.int32)
        end = jnp.int32(0)
        for n in range(lengths.shape[0]):
            end = end + lengths[n]
            start = jnp.where(q_pos >= end, end, start)
        k_pos = lax.broadcasted_iota(jnp.int32, (piece, span), 1)
        bias = jnp.where((k_pos <= q_pos) & (k_pos >= start), 0.0, -1e30)
        scores = lax.dot_general(
            rows, keys, (((1,), (1,)), ((), ())), preferred_element_type=jnp.float32
        )
        scores = scores.reshape(heads_here, piece, span) * factor + bias[None]
        highest = jnp.max(scores, axis=2, keepdims=True)
        weights = jnp.exp2(scores - highest)
        total = jnp.sum(weights, axis=2, keepdims=True)
        summed = jnp.dot(
            weights.reshape(heads_here * piece, span).astype(jnp.bfloat16), vals,
            preferred_element_type=jnp.float32,
        ).reshape(heads_here, piece, HD)
        result = (summed / total).astype(att.dtype)
        for h in range(heads_here):
            att[s * piece:(s + 1) * piece, h * HD:(h + 1) * HD] = result[h]

    def product(t, c):
        rows = att[pl.ds(pl.multiple_of(t * out_rows, out_rows), out_rows), :]
        cols = w_buf[:, pl.ds(pl.multiple_of(c * cw, cw), cw)]
        return jnp.dot(rows.astype(jnp.bfloat16), cols, preferred_element_type=jnp.float32)

    def r_copy(k):
        return pltpu.make_async_remote_copy(
            src_ref=out_r.at[k], dst_ref=in_r.at[k],
            send_sem=r_send.at[k], recv_sem=r_recv.at[k],
            device_id=(me, lax.rem(z + 1, T)), device_id_type=MESH,
        )

    def l_copy(k):
        return pltpu.make_async_remote_copy(
            src_ref=out_l.at[k], dst_ref=in_l.at[k],
            send_sem=l_send.at[k], recv_sem=l_recv.at[k],
            device_id=(me, lax.rem(z + T - 1, T)), device_id_type=MESH,
        )

    def far_product(t, c):
        rows = att_far[pl.ds(pl.multiple_of(t * out_rows, out_rows), out_rows), :]
        rows = rows.astype(jnp.bfloat16)
        per_chunk = cw // far_cols
        return jnp.concatenate(
            [
                jnp.dot(
                    rows, w_far[(c - early_chunks) * per_chunk + n],
                    preferred_element_type=jnp.float32,
                )
                for n in range(per_chunk)
            ],
            axis=1,
        )

    def add_to(ref, index, more):
        ref[index] = (ref[index].astype(jnp.float32) + more).astype(jnp.bfloat16)

    def place_of(k):
        return k % half // early_chunks, k // half * early_chunks + k % early_chunks

    def right(k):
        n, c = place_of(k)
        t = T - 1 - n
        late = k >= half

        @pl.when((z < t) & ((z > 0) | (k < half)))
        def _():
            out_r[k] = product(t, c).astype(jnp.bfloat16)

            @pl.when((z > 1) | ((z == 1) & (k < half)))
            def _():
                r_copy(k).wait_recv()
                add_to(out_r, k, in_r[k].astype(jnp.float32))

            @pl.when((z == 1) & late)
            def _():
                add_to(out_r, k, far_product(t, c))

            r_copy(k).start()

    def left(k):
        t, c = place_of(k)
        late = k >= half

        @pl.when((z > t) & ((z < T - 1) | (k < half)))
        def _():
            out_l[k] = product(t, c).astype(jnp.bfloat16)

            @pl.when((z < T - 2) | ((z == T - 2) & (k < half)))
            def _():
                l_copy(k).wait_recv()
                add_to(out_l, k, in_l[k].astype(jnp.float32))

            @pl.when((z == T - 2) & late)
            def _():
                add_to(out_l, k, far_product(t, c))

            l_copy(k).start()

    def step(k, carry):
        k_r = k - LAG * jnp.maximum(z - 1, 0)
        k_l = k - LAG * jnp.maximum(T - 2 - z, 0)

        def go_right():
            @pl.when((k_r >= 0) & (k_r < 2 * half))
            def _():
                right(k_r)

        def go_left():
            @pl.when((k_l >= 0) & (k_l < 2 * half))
            def _():
                left(k_l)

        @pl.when(z < T // 2)
        def _():
            go_right()
            go_left()

        @pl.when(z >= T // 2)
        def _():
            go_left()
            go_right()

        return carry

    def send_rows(t):
        @pl.when((low & (t > 0)) | (high & (t < T - 1)))
        def _():
            row_copy(t).start()

    early = (T - 1, 0)
    for t in early:
        for s in range(t * per_dest, (t + 1) * per_dest):
            attend(s)
    load_w.wait()
    lax.fori_loop(0, early_chunks, step, 0)
    for t in range(T):
        if t not in early:
            for s in range(t * per_dest, (t + 1) * per_dest):
                attend(s)

    @pl.when(next_low | next_high)
    def _():
        for i in range(1, G // 2):
            owner = lax.rem(me + G - 2 * i, G)
            peer_copy(i, owner).wait_recv()
            pass_copy(i, owner).start()

    for t in range(T):
        send_rows(t)
    lax.fori_loop(early_chunks, half, step, 0)

    @pl.when(next_low | next_high)
    def _():
        for i in range(G // 2):
            pass_copy(i, lax.rem(partner + G - 2 * i, G)).wait_recv()
        for t in range(T):
            @pl.when((next_low & (t > 0)) | (next_high & (t < T - 1)))
            def _():
                row_copy(t).wait_recv()

    lax.fori_loop(half, 2 * half + LAG * (T - 2), step, 0)

    def finish(c, carry):
        cols = pl.ds(pl.multiple_of(c * cw, cw), cw)
        late = c >= early_chunks
        base = c // early_chunks * half + c % early_chunks

        def add_out(more):
            out_ref[:, cols] = (out_ref[:, cols].astype(jnp.float32) + more).astype(jnp.bfloat16)

        out_ref[:, cols] = product(z, c).astype(jnp.bfloat16)

        @pl.when((next_low | next_high) & late)
        def _():
            add_out(far_product(z, c))

        @pl.when((z < T - 2) | ((z == T - 2) & (c < early_chunks)))
        def _():
            k = base + z * early_chunks
            l_copy(k).wait_recv()
            add_out(in_l[k].astype(jnp.float32))

        @pl.when((z > 1) | ((z == 1) & (c < early_chunks)))
        def _():
            k = base + (T - 1 - z) * early_chunks
            r_copy(k).wait_recv()
            add_out(in_r[k].astype(jnp.float32))

        return carry

    lax.fori_loop(0, CHUNKS, finish, 0)

    for i in range(1, G):
        q_copy(i, me).wait_send()
    for which in both:
        for i in range(1, G // 2):
            once_copy(which, i, me).wait_send()
        for i in range(G // 2):
            partner_copy(which, i, me).wait_send()

    @pl.when(low | high)
    def _():
        far_copy().wait_send()
        for t in range(T):
            @pl.when((low & (t > 0)) | (high & (t < T - 1)))
            def _():
                row_copy(t).wait_send()

    @pl.when(next_low | next_high)
    def _():
        for i in range(1, G // 2):
            peer_copy(i, me).wait_send()
        for i in range(G // 2):
            pass_copy(i, lax.rem(me + G - 2 * i, G)).wait_send()

    def drain(k, carry):
        n, _ = place_of(k)

        @pl.when((z < T - 1 - n) & ((z > 0) | (k < half)))
        def _():
            r_copy(k).wait_send()

        @pl.when((z > n) & ((z < T - 1) | (k < half)))
        def _():
            l_copy(k).wait_send()

        return carry

    lax.fori_loop(0, 2 * half, drain, 0)


def local(queries, keys, values, lengths, assignment, out_weight):
    G = lax.axis_size("dp")
    T = lax.axis_size("tensor")
    tok_rows, q_width = queries.shape
    n_cols = out_weight.shape[1]
    piece = tok_rows // G
    out_rows = tok_rows // T
    cw = n_cols // CHUNKS
    slots = (T - 1) * CHUNKS
    parts = CHUNKS
    far_cols = CHUNKS // 2 * cw // parts
    att_type = jnp.bfloat16 if piece % 16 == 0 else jnp.float32
    smem = pl.BlockSpec(memory_space=pltpu.SMEM)
    hbm = pl.BlockSpec(memory_space=pl.ANY)
    dma = pltpu.SemaphoreType.DMA
    bf16 = jnp.bfloat16

    def body(*refs):
        kernel(G, T, *refs)

    return pl.pallas_call(
        body,
        out_shape=jax.ShapeDtypeStruct((out_rows, n_cols), bf16),
        in_specs=[smem, smem, hbm, hbm, hbm, hbm],
        out_specs=pl.BlockSpec(memory_space=pltpu.VMEM),
        scratch_shapes=[
            pltpu.VMEM((tok_rows, q_width), bf16),
            pltpu.VMEM((G, piece, q_width), bf16),
            pltpu.VMEM((G, piece, q_width), bf16),
            pltpu.VMEM((G, tok_rows, HD), bf16),
            pltpu.VMEM((G, tok_rows, HD), bf16),
            pltpu.VMEM(out_weight.shape, bf16),
            pltpu.VMEM((tok_rows, q_width), att_type),
            pltpu.VMEM((slots, out_rows, cw), bf16),
            pltpu.VMEM((slots, out_rows, cw), bf16),
            pltpu.VMEM((slots, out_rows, cw), bf16),
            pltpu.VMEM((slots, out_rows, cw), bf16),
            dma, dma, dma((2,)),
            dma((G,)), dma((G,)), dma((G,)), dma((G,)), dma((G,)), dma((G,)),
            dma((slots,)), dma((slots,)), dma((slots,)), dma((slots,)),
            pltpu.VMEM((parts, q_width, far_cols), bf16),
            pltpu.VMEM((tok_rows, q_width), att_type),
            dma, dma, dma((G,)), dma((G,)), dma((T,)), dma((T,)),
        ],
        compiler_params=pltpu.CompilerParams(
            collective_id=0, has_side_effects=True, vmem_limit_bytes=60 << 20
        ),
    )(lengths, assignment, queries, keys, values, out_weight)


def solution(mesh):
    in_specs = (P("dp", "tensor"), P("dp", None), P("dp", None), P(), P(), P("tensor", None))
    out_specs = P(("dp", "tensor"), None)
    return jax.shard_map(local, mesh=mesh, in_specs=in_specs, out_specs=out_specs, check_vma=False)
```

```python
import math

import jax
import jax.numpy as jnp
from jax import lax
from jax.experimental import pallas as pl
from jax.experimental.pallas import tpu as pltpu
from jax.sharding import PartitionSpec as P

HD = 128
HEADS = 24
KV_HEADS = 4
MESH = pl.DeviceIdType.MESH
CHUNKS = 8
LAG = 3


def kernel(
    G, T, lengths, assignment, q_hbm, k_hbm, v_hbm, w_hbm, out_ref,
    q_all, q_stage, q_buf, k_buf, v_buf, w_buf, att, in_r, in_l, out_r, out_l,
    load_sem, w_sem, own_sem, k_send, k_recv, v_send, v_recv, q_send, q_recv,
    r_send, r_recv, l_send, l_recv,
    w_far, att_far, far_send, far_recv, near_send, near_recv, row_send, row_recv,
):
    me = lax.axis_index("dp")
    z = lax.axis_index("tensor")
    tok_rows, q_width = q_all.shape
    heads_here = q_width // HD
    piece = tok_rows // G
    per_dest = G // T
    out_rows = tok_rows // T
    n_cols = w_buf.shape[1]
    cw = n_cols // CHUNKS
    early_chunks = CHUNKS // 2
    half = (T - 1) * early_chunks
    parts, far_rows, far_cols = w_far.shape
    share_rows = far_rows * parts // G
    low, high = z == 0, z == T - 1
    next_low, next_high = z == 1, z == T - 2
    partner = me + 1 - 2 * (me % 2)
    kv_head = z * heads_here // (HEADS // KV_HEADS)
    kv_cols = pl.ds(pl.multiple_of(kv_head * HD, HD), HD)

    load_q = pltpu.make_async_copy(q_hbm, q_all, load_sem)
    load_q.start()
    barrier = pltpu.get_barrier_semaphore()
    for i in range(1, G):
        pl.semaphore_signal(
            barrier, inc=1, device_id=(lax.rem(me + i, G), z), device_id_type=MESH
        )
    for i in range(1, T):
        pl.semaphore_signal(
            barrier, inc=1, device_id=(me, lax.rem(z + i, T)), device_id_type=MESH
        )
    own_k = pltpu.make_async_copy(k_hbm.at[:, kv_cols], k_buf.at[me], own_sem.at[0])
    own_v = pltpu.make_async_copy(v_hbm.at[:, kv_cols], v_buf.at[me], own_sem.at[1])
    own_k.start()
    own_v.start()
    load_w = pltpu.make_async_copy(w_hbm, w_buf, w_sem)
    load_w.start()
    load_q.wait()
    place = lax.broadcasted_iota(jnp.int32, (tok_rows, 1), 0)
    source_row = jnp.zeros((tok_rows, 1), jnp.int32)
    for g in range(G):
        here = (place >= g * piece) & (place < (g + 1) * piece)
        source_row = source_row + jnp.where(here, (assignment[me, g] - g) * piece + place, 0)
    chosen = (lax.broadcasted_iota(jnp.int32, (tok_rows, tok_rows), 1) == source_row)
    picked = jnp.dot(
        chosen.astype(jnp.float32).astype(jnp.bfloat16), q_all[...],
        preferred_element_type=jnp.float32,
    ).astype(jnp.bfloat16)
    for g in range(G):
        q_stage[g] = picked[g * piece:(g + 1) * piece]
    q_buf[me] = q_stage[me]
    pl.semaphore_wait(barrier, G - 1 + T - 1)

    def q_copy(i, source):
        return pltpu.make_async_remote_copy(
            src_ref=q_stage.at[lax.rem(me + i, G)], dst_ref=q_buf.at[source],
            send_sem=q_send.at[i], recv_sem=q_recv.at[i],
            device_id=(lax.rem(me + i, G), z), device_id_type=MESH,
        )

    def once_copy(which, i, source):
        hbm, buf, send, recv = which
        return pltpu.make_async_remote_copy(
            src_ref=hbm.at[:, kv_cols], dst_ref=buf.at[source],
            send_sem=send.at[i], recv_sem=recv.at[i],
            device_id=(lax.rem(me + 2 * i, G), z), device_id_type=MESH,
        )

    def partner_copy(which, i, source):
        hbm, buf, send, recv = which
        return pltpu.make_async_remote_copy(
            src_ref=hbm.at[:, kv_cols] if i == 0 else buf.at[source], dst_ref=buf.at[source],
            send_sem=send.at[G // 2 + i], recv_sem=recv.at[G // 2 + i],
            device_id=(partner, z), device_id_type=MESH,
        )

    both = ((k_hbm, k_buf, k_send, k_recv), (v_hbm, v_buf, v_send, v_recv))

    def share(j):
        rows = pl.ds(pl.multiple_of((j // parts) * share_rows, share_rows), share_rows)
        return w_far.at[j % parts, rows, :]

    def far_copy():
        rows = pl.ds(pl.multiple_of((me // parts) * share_rows, share_rows), share_rows)
        first = early_chunks * cw + (me % parts) * far_cols
        cols = pl.ds(pl.multiple_of(first, far_cols), far_cols)
        return pltpu.make_async_remote_copy(
            src_ref=w_hbm.at[rows, cols], dst_ref=share(me),
            send_sem=far_send, recv_sem=far_recv,
            device_id=(me, jnp.where(z == 0, 1, T - 2)), device_id_type=MESH,
        )

    def peer_copy(i, owner):
        return pltpu.make_async_remote_copy(
            src_ref=share(owner), dst_ref=share(owner),
            send_sem=near_send.at[i], recv_sem=near_recv.at[i],
            device_id=(lax.rem(me + 2 * i, G), z), device_id_type=MESH,
        )

    def pass_copy(i, owner):
        return pltpu.make_async_remote_copy(
            src_ref=share(owner), dst_ref=share(owner),
            send_sem=near_send.at[G // 2 + i], recv_sem=near_recv.at[G // 2 + i],
            device_id=(partner, z), device_id_type=MESH,
        )

    def row_copy(t):
        rows = pl.ds(t * out_rows, out_rows)
        return pltpu.make_async_remote_copy(
            src_ref=att.at[rows, :], dst_ref=att_far.at[rows, :],
            send_sem=row_send.at[t], recv_sem=row_recv.at[t],
            device_id=(me, jnp.where(z == 0, 1, T - 2)), device_id_type=MESH,
        )

    @pl.when(low | high)
    def _():
        far_copy().start()

    for which in both:
        for i in range(1, G // 2):
            once_copy(which, i, me).start()
    for which in both:
        partner_copy(which, 0, me).start()
    for i in range(1, G):
        q_copy(i, me).start()
    own_k.wait()
    own_v.wait()
    for which in both:
        for i in range(1, G // 2):
            source = lax.rem(me + G - 2 * i, G)
            once_copy(which, i, source).wait_recv()
            partner_copy(which, i, source).start()
    for which in both:
        for i in range(G // 2):
            partner_copy(which, i, lax.rem(partner + G - 2 * i, G)).wait_recv()
    for i in range(1, G):
        q_copy(i, lax.rem(me + G - i, G)).wait_recv()

    @pl.when(next_low | next_high)
    def _():
        far_copy().wait_recv()
        for i in range(1, G // 2):
            peer_copy(i, me).start()
        pass_copy(0, me).start()

    factor = HD ** (-0.5) * math.log2(math.e)

    def attend(s):
        span = (s + 1) * tok_rows
        q_rows = q_buf[s]
        if piece % 16:
            q_rows = q_rows.astype(jnp.float32)
        rows = jnp.concatenate(
            [q_rows[:, h * HD:(h + 1) * HD] for h in range(heads_here)], axis=0
        ).astype(jnp.bfloat16)
        keys = k_buf[:s + 1].reshape(span, HD)
        vals = v_buf[:s + 1].reshape(span, HD)
        q_pos = (
            s * tok_rows + assignment[s, me] * piece
            + lax.broadcasted_iota(jnp.int32, (piece, 1), 0)
        )
        start = jnp.zeros((piece, 1), jnp.int32)
        end = jnp.int32(0)
        for n in range(lengths.shape[0]):
            end = end + lengths[n]
            start = jnp.where(q_pos >= end, end, start)
        k_pos = lax.broadcasted_iota(jnp.int32, (piece, span), 1)
        bias = jnp.where((k_pos <= q_pos) & (k_pos >= start), 0.0, -1e30)
        scores = lax.dot_general(
            rows, keys, (((1,), (1,)), ((), ())), preferred_element_type=jnp.float32
        )
        scores = scores.reshape(heads_here, piece, span) * factor + bias[None]
        highest = jnp.max(scores, axis=2, keepdims=True)
        weights = jnp.exp2(scores - highest)
        total = jnp.sum(weights, axis=2, keepdims=True)
        summed = jnp.dot(
            weights.reshape(heads_here * piece, span).astype(jnp.bfloat16), vals,
            preferred_element_type=jnp.float32,
        ).reshape(heads_here, piece, HD)
        result = (summed / total).astype(att.dtype)
        for h in range(heads_here):
            att[s * piece:(s + 1) * piece, h * HD:(h + 1) * HD] = result[h]

    def product(t, c):
        rows = att[pl.ds(pl.multiple_of(t * out_rows, out_rows), out_rows), :]
        cols = w_buf[:, pl.ds(pl.multiple_of(c * cw, cw), cw)]
        return jnp.dot(rows.astype(jnp.bfloat16), cols, preferred_element_type=jnp.float32)

    def r_copy(k):
        return pltpu.make_async_remote_copy(
            src_ref=out_r.at[k], dst_ref=in_r.at[k],
            send_sem=r_send.at[k], recv_sem=r_recv.at[k],
            device_id=(me, lax.rem(z + 1, T)), device_id_type=MESH,
        )

    def l_copy(k):
        return pltpu.make_async_remote_copy(
            src_ref=out_l.at[k], dst_ref=in_l.at[k],
            send_sem=l_send.at[k], recv_sem=l_recv.at[k],
            device_id=(me, lax.rem(z + T - 1, T)), device_id_type=MESH,
        )

    def far_product(t, c):
        rows = att_far[pl.ds(pl.multiple_of(t * out_rows, out_rows), out_rows), :]
        rows = rows.astype(jnp.bfloat16)
        per_chunk = cw // far_cols
        return jnp.concatenate(
            [
                jnp.dot(
                    rows, w_far[(c - early_chunks) * per_chunk + n],
                    preferred_element_type=jnp.float32,
                )
                for n in range(per_chunk)
            ],
            axis=1,
        )

    def add_to(ref, index, more):
        ref[index] = (ref[index].astype(jnp.float32) + more).astype(jnp.bfloat16)

    def place_of(k):
        return k % half // early_chunks, k // half * early_chunks + k % early_chunks

    def right(k):
        n, c = place_of(k)
        t = T - 1 - n
        late = k >= half

        @pl.when((z < t) & ((z > 0) | (k < half)))
        def _():
            out_r[k] = product(t, c).astype(jnp.bfloat16)

            @pl.when((z > 1) | ((z == 1) & (k < half)))
            def _():
                r_copy(k).wait_recv()
                add_to(out_r, k, in_r[k].astype(jnp.float32))

            @pl.when((z == 1) & late)
            def _():
                add_to(out_r, k, far_product(t, c))

            r_copy(k).start()

    def left(k):
        t, c = place_of(k)
        late = k >= half

        @pl.when((z > t) & ((z < T - 1) | (k < half)))
        def _():
            out_l[k] = product(t, c).astype(jnp.bfloat16)

            @pl.when((z < T - 2) | ((z == T - 2) & (k < half)))
            def _():
                l_copy(k).wait_recv()
                add_to(out_l, k, in_l[k].astype(jnp.float32))

            @pl.when((z == T - 2) & late)
            def _():
                add_to(out_l, k, far_product(t, c))

            l_copy(k).start()

    def step(k, carry):
        k_r = k - LAG * jnp.maximum(z - 1, 0)
        k_l = k - LAG * jnp.maximum(T - 2 - z, 0)

        def go_right():
            @pl.when((k_r >= 0) & (k_r < 2 * half))
            def _():
                right(k_r)

        def go_left():
            @pl.when((k_l >= 0) & (k_l < 2 * half))
            def _():
                left(k_l)

        @pl.when(z < T // 2)
        def _():
            go_right()
            go_left()

        @pl.when(z >= T // 2)
        def _():
            go_left()
            go_right()

        return carry

    def send_rows(t):
        @pl.when((low & (t > 0)) | (high & (t < T - 1)))
        def _():
            row_copy(t).start()

    early = (T - 1, 0)
    for t in early:
        for s in range(t * per_dest, (t + 1) * per_dest):
            attend(s)
    load_w.wait()
    lax.fori_loop(0, early_chunks, step, 0)
    for t in range(T):
        if t not in early:
            for s in range(t * per_dest, (t + 1) * per_dest):
                attend(s)

    for t in range(T):
        send_rows(t)
    lax.fori_loop(early_chunks, half, step, 0)

    @pl.when(next_low | next_high)
    def _():
        for i in range(1, G // 2):
            owner = lax.rem(me + G - 2 * i, G)
            peer_copy(i, owner).wait_recv()
            pass_copy(i, owner).start()

    @pl.when(next_low | next_high)
    def _():
        for i in range(G // 2):
            pass_copy(i, lax.rem(partner + G - 2 * i, G)).wait_recv()
        for t in range(T):
            @pl.when((next_low & (t > 0)) | (next_high & (t < T - 1)))
            def _():
                row_copy(t).wait_recv()

    lax.fori_loop(half, 2 * half + LAG * (T - 2), step, 0)

    def finish(c, carry):
        cols = pl.ds(pl.multiple_of(c * cw, cw), cw)
        late = c >= early_chunks
        base = c // early_chunks * half + c % early_chunks

        def add_out(more):
            out_ref[:, cols] = (out_ref[:, cols].astype(jnp.float32) + more).astype(jnp.bfloat16)

        out_ref[:, cols] = product(z, c).astype(jnp.bfloat16)

        @pl.when((next_low | next_high) & late)
        def _():
            add_out(far_product(z, c))

        @pl.when((z < T - 2) | ((z == T - 2) & (c < early_chunks)))
        def _():
            k = base + z * early_chunks
            l_copy(k).wait_recv()
            add_out(in_l[k].astype(jnp.float32))

        @pl.when((z > 1) | ((z == 1) & (c < early_chunks)))
        def _():
            k = base + (T - 1 - z) * early_chunks
            r_copy(k).wait_recv()
            add_out(in_r[k].astype(jnp.float32))

        return carry

    lax.fori_loop(0, CHUNKS, finish, 0)

    for i in range(1, G):
        q_copy(i, me).wait_send()
    for which in both:
        for i in range(1, G // 2):
            once_copy(which, i, me).wait_send()
        for i in range(G // 2):
            partner_copy(which, i, me).wait_send()

    @pl.when(low | high)
    def _():
        far_copy().wait_send()
        for t in range(T):
            @pl.when((low & (t > 0)) | (high & (t < T - 1)))
            def _():
                row_copy(t).wait_send()

    @pl.when(next_low | next_high)
    def _():
        for i in range(1, G // 2):
            peer_copy(i, me).wait_send()
        for i in range(G // 2):
            pass_copy(i, lax.rem(me + G - 2 * i, G)).wait_send()

    def drain(k, carry):
        n, _ = place_of(k)

        @pl.when((z < T - 1 - n) & ((z > 0) | (k < half)))
        def _():
            r_copy(k).wait_send()

        @pl.when((z > n) & ((z < T - 1) | (k < half)))
        def _():
            l_copy(k).wait_send()

        return carry

    lax.fori_loop(0, 2 * half, drain, 0)


def local(queries, keys, values, lengths, assignment, out_weight):
    G = lax.axis_size("dp")
    T = lax.axis_size("tensor")
    tok_rows, q_width = queries.shape
    n_cols = out_weight.shape[1]
    piece = tok_rows // G
    out_rows = tok_rows // T
    cw = n_cols // CHUNKS
    slots = (T - 1) * CHUNKS
    parts = CHUNKS
    far_cols = CHUNKS // 2 * cw // parts
    att_type = jnp.bfloat16 if piece % 16 == 0 else jnp.float32
    smem = pl.BlockSpec(memory_space=pltpu.SMEM)
    hbm = pl.BlockSpec(memory_space=pl.ANY)
    dma = pltpu.SemaphoreType.DMA
    bf16 = jnp.bfloat16

    def body(*refs):
        kernel(G, T, *refs)

    return pl.pallas_call(
        body,
        out_shape=jax.ShapeDtypeStruct((out_rows, n_cols), bf16),
        in_specs=[smem, smem, hbm, hbm, hbm, hbm],
        out_specs=pl.BlockSpec(memory_space=pltpu.VMEM),
        scratch_shapes=[
            pltpu.VMEM((tok_rows, q_width), bf16),
            pltpu.VMEM((G, piece, q_width), bf16),
            pltpu.VMEM((G, piece, q_width), bf16),
            pltpu.VMEM((G, tok_rows, HD), bf16),
            pltpu.VMEM((G, tok_rows, HD), bf16),
            pltpu.VMEM(out_weight.shape, bf16),
            pltpu.VMEM((tok_rows, q_width), att_type),
            pltpu.VMEM((slots, out_rows, cw), bf16),
            pltpu.VMEM((slots, out_rows, cw), bf16),
            pltpu.VMEM((slots, out_rows, cw), bf16),
            pltpu.VMEM((slots, out_rows, cw), bf16),
            dma, dma, dma((2,)),
            dma((G,)), dma((G,)), dma((G,)), dma((G,)), dma((G,)), dma((G,)),
            dma((slots,)), dma((slots,)), dma((slots,)), dma((slots,)),
            pltpu.VMEM((parts, q_width, far_cols), bf16),
            pltpu.VMEM((tok_rows, q_width), att_type),
            dma, dma, dma((G,)), dma((G,)), dma((T,)), dma((T,)),
        ],
        compiler_params=pltpu.CompilerParams(
            collective_id=0, has_side_effects=True, vmem_limit_bytes=60 << 20
        ),
    )(lengths, assignment, queries, keys, values, out_weight)


def solution(mesh):
    in_specs = (P("dp", "tensor"), P("dp", None), P("dp", None), P(), P(), P("tensor", None))
    out_specs = P(("dp", "tensor"), None)
    return jax.shard_map(local, mesh=mesh, in_specs=in_specs, out_specs=out_specs, check_vma=False)
```

```python
import math

import jax
import jax.numpy as jnp
from jax import lax
from jax.experimental import pallas as pl
from jax.experimental.pallas import tpu as pltpu
from jax.sharding import PartitionSpec as P

HD = 128
HEADS = 24
KV_HEADS = 4
MESH = pl.DeviceIdType.MESH
CHUNKS = 8
LAG = 3


def kernel(
    G, T, lengths, assignment, q_hbm, k_hbm, v_hbm, w_hbm, out_ref,
    q_all, q_stage, q_buf, k_buf, v_buf, w_buf, att, in_r, in_l, out_r, out_l,
    load_sem, w_sem, own_sem, k_send, k_recv, v_send, v_recv, q_send, q_recv,
    r_send, r_recv, l_send, l_recv,
    w_far, att_far, far_send, far_recv, near_send, near_recv, row_send, row_recv,
):
    me = lax.axis_index("dp")
    z = lax.axis_index("tensor")
    tok_rows, q_width = q_all.shape
    heads_here = q_width // HD
    piece = tok_rows // G
    per_dest = G // T
    out_rows = tok_rows // T
    n_cols = w_buf.shape[1]
    cw = n_cols // CHUNKS
    early_chunks = CHUNKS // 2
    half = (T - 1) * early_chunks
    parts, far_rows, far_cols = w_far.shape
    share_rows = far_rows * parts // G
    low, high = z == 0, z == T - 1
    next_low, next_high = z == 1, z == T - 2
    partner = me + 1 - 2 * (me % 2)
    kv_head = z * heads_here // (HEADS // KV_HEADS)
    kv_cols = pl.ds(pl.multiple_of(kv_head * HD, HD), HD)

    load_q = pltpu.make_async_copy(q_hbm, q_all, load_sem)
    load_q.start()
    barrier = pltpu.get_barrier_semaphore()
    for i in range(1, G):
        pl.semaphore_signal(
            barrier, inc=1, device_id=(lax.rem(me + i, G), z), device_id_type=MESH
        )
    for i in range(1, T):
        pl.semaphore_signal(
            barrier, inc=1, device_id=(me, lax.rem(z + i, T)), device_id_type=MESH
        )
    own_k = pltpu.make_async_copy(k_hbm.at[:, kv_cols], k_buf.at[me], own_sem.at[0])
    own_v = pltpu.make_async_copy(v_hbm.at[:, kv_cols], v_buf.at[me], own_sem.at[1])
    own_k.start()
    own_v.start()
    load_w = pltpu.make_async_copy(w_hbm, w_buf, w_sem)
    load_w.start()
    load_q.wait()
    place = lax.broadcasted_iota(jnp.int32, (tok_rows, 1), 0)
    source_row = jnp.zeros((tok_rows, 1), jnp.int32)
    for g in range(G):
        here = (place >= g * piece) & (place < (g + 1) * piece)
        source_row = source_row + jnp.where(here, (assignment[me, g] - g) * piece + place, 0)
    chosen = (lax.broadcasted_iota(jnp.int32, (tok_rows, tok_rows), 1) == source_row)
    picked = jnp.dot(
        chosen.astype(jnp.float32).astype(jnp.bfloat16), q_all[...],
        preferred_element_type=jnp.float32,
    ).astype(jnp.bfloat16)
    for g in range(G):
        q_stage[g] = picked[g * piece:(g + 1) * piece]
    q_buf[me] = q_stage[me]
    pl.semaphore_wait(barrier, G - 1 + T - 1)

    def q_copy(i, source):
        return pltpu.make_async_remote_copy(
            src_ref=q_stage.at[lax.rem(me + i, G)], dst_ref=q_buf.at[source],
            send_sem=q_send.at[i], recv_sem=q_recv.at[i],
            device_id=(lax.rem(me + i, G), z), device_id_type=MESH,
        )

    def once_copy(which, i, source):
        hbm, buf, send, recv = which
        return pltpu.make_async_remote_copy(
            src_ref=hbm.at[:, kv_cols], dst_ref=buf.at[source],
            send_sem=send.at[i], recv_sem=recv.at[i],
            device_id=(lax.rem(me + 2 * i, G), z), device_id_type=MESH,
        )

    def partner_copy(which, i, source):
        hbm, buf, send, recv = which
        return pltpu.make_async_remote_copy(
            src_ref=hbm.at[:, kv_cols] if i == 0 else buf.at[source], dst_ref=buf.at[source],
            send_sem=send.at[G // 2 + i], recv_sem=recv.at[G // 2 + i],
            device_id=(partner, z), device_id_type=MESH,
        )

    both = ((k_hbm, k_buf, k_send, k_recv), (v_hbm, v_buf, v_send, v_recv))

    def share(j):
        rows = pl.ds(pl.multiple_of((j // parts) * share_rows, share_rows), share_rows)
        return w_far.at[j % parts, rows, :]

    def far_copy():
        rows = pl.ds(pl.multiple_of((me // parts) * share_rows, share_rows), share_rows)
        first = early_chunks * cw + (me % parts) * far_cols
        cols = pl.ds(pl.multiple_of(first, far_cols), far_cols)
        return pltpu.make_async_remote_copy(
            src_ref=w_hbm.at[rows, cols], dst_ref=share(me),
            send_sem=far_send, recv_sem=far_recv,
            device_id=(me, jnp.where(z == 0, 1, T - 2)), device_id_type=MESH,
        )

    def peer_copy(i, owner):
        return pltpu.make_async_remote_copy(
            src_ref=share(owner), dst_ref=share(owner),
            send_sem=near_send.at[i], recv_sem=near_recv.at[i],
            device_id=(lax.rem(me + 2 * i, G), z), device_id_type=MESH,
        )

    def pass_copy(i, owner):
        return pltpu.make_async_remote_copy(
            src_ref=share(owner), dst_ref=share(owner),
            send_sem=near_send.at[G // 2 + i], recv_sem=near_recv.at[G // 2 + i],
            device_id=(partner, z), device_id_type=MESH,
        )

    def row_copy(t):
        rows = pl.ds(t * out_rows, out_rows)
        return pltpu.make_async_remote_copy(
            src_ref=att.at[rows, :], dst_ref=att_far.at[rows, :],
            send_sem=row_send.at[t], recv_sem=row_recv.at[t],
            device_id=(me, jnp.where(z == 0, 1, T - 2)), device_id_type=MESH,
        )

    @pl.when(low | high)
    def _():
        far_copy().start()

    for which in both:
        for i in range(1, G // 2):
            once_copy(which, i, me).start()
    for which in both:
        partner_copy(which, 0, me).start()
    for i in range(1, G):
        q_copy(i, me).start()
    own_k.wait()
    own_v.wait()
    for which in both:
        for i in range(1, G // 2):
            source = lax.rem(me + G - 2 * i, G)
            once_copy(which, i, source).wait_recv()
            partner_copy(which, i, source).start()
    for which in both:
        for i in range(G // 2):
            partner_copy(which, i, lax.rem(partner + G - 2 * i, G)).wait_recv()
    for i in range(1, G):
        q_copy(i, lax.rem(me + G - i, G)).wait_recv()

    @pl.when(next_low | next_high)
    def _():
        far_copy().wait_recv()
        for i in range(1, G // 2):
            peer_copy(i, me).start()
        pass_copy(0, me).start()

    factor = HD ** (-0.5) * math.log2(math.e)

    def attend(s):
        span = (s + 1) * tok_rows
        q_rows = q_buf[s]
        if piece % 16:
            q_rows = q_rows.astype(jnp.float32)
        rows = jnp.concatenate(
            [q_rows[:, h * HD:(h + 1) * HD] for h in range(heads_here)], axis=0
        ).astype(jnp.bfloat16)
        keys = k_buf[:s + 1].reshape(span, HD)
        vals = v_buf[:s + 1].reshape(span, HD)
        q_pos = (
            s * tok_rows + assignment[s, me] * piece
            + lax.broadcasted_iota(jnp.int32, (piece, 1), 0)
        )
        start = jnp.zeros((piece, 1), jnp.int32)
        end = jnp.int32(0)
        for n in range(lengths.shape[0]):
            end = end + lengths[n]
            start = jnp.where(q_pos >= end, end, start)
        k_pos = lax.broadcasted_iota(jnp.int32, (piece, span), 1)
        bias = jnp.where((k_pos <= q_pos) & (k_pos >= start), 0.0, -1e30)
        scores = lax.dot_general(
            rows, keys, (((1,), (1,)), ((), ())), preferred_element_type=jnp.float32
        )
        scores = scores.reshape(heads_here, piece, span) * factor + bias[None]
        highest = jnp.max(scores, axis=2, keepdims=True)
        weights = jnp.exp2(scores - highest)
        total = jnp.sum(weights, axis=2, keepdims=True)
        summed = jnp.dot(
            weights.reshape(heads_here * piece, span).astype(jnp.bfloat16), vals,
            preferred_element_type=jnp.float32,
        ).reshape(heads_here, piece, HD)
        result = (summed / total).astype(att.dtype)
        for h in range(heads_here):
            att[s * piece:(s + 1) * piece, h * HD:(h + 1) * HD] = result[h]

    def product(t, c):
        rows = att[pl.ds(pl.multiple_of(t * out_rows, out_rows), out_rows), :]
        cols = w_buf[:, pl.ds(pl.multiple_of(c * cw, cw), cw)]
        return jnp.dot(rows.astype(jnp.bfloat16), cols, preferred_element_type=jnp.float32)

    def r_copy(k):
        return pltpu.make_async_remote_copy(
            src_ref=out_r.at[k], dst_ref=in_r.at[k],
            send_sem=r_send.at[k], recv_sem=r_recv.at[k],
            device_id=(me, lax.rem(z + 1, T)), device_id_type=MESH,
        )

    def l_copy(k):
        return pltpu.make_async_remote_copy(
            src_ref=out_l.at[k], dst_ref=in_l.at[k],
            send_sem=l_send.at[k], recv_sem=l_recv.at[k],
            device_id=(me, lax.rem(z + T - 1, T)), device_id_type=MESH,
        )

    def far_product(t, c):
        rows = att_far[pl.ds(pl.multiple_of(t * out_rows, out_rows), out_rows), :]
        rows = rows.astype(jnp.bfloat16)
        per_chunk = cw // far_cols
        return jnp.concatenate(
            [
                jnp.dot(
                    rows, w_far[(c - early_chunks) * per_chunk + n],
                    preferred_element_type=jnp.float32,
                )
                for n in range(per_chunk)
            ],
            axis=1,
        )

    def add_to(ref, index, more):
        ref[index] = (ref[index].astype(jnp.float32) + more).astype(jnp.bfloat16)

    def place_of(k):
        return k % half // early_chunks, k // half * early_chunks + k % early_chunks

    def right(k):
        n, c = place_of(k)
        t = T - 1 - n
        late = k >= half

        @pl.when((z < t) & ((z > 0) | (k < half)))
        def _():
            out_r[k] = product(t, c).astype(jnp.bfloat16)

            @pl.when((z > 1) | ((z == 1) & (k < half)))
            def _():
                r_copy(k).wait_recv()
                add_to(out_r, k, in_r[k].astype(jnp.float32))

            @pl.when((z == 1) & late)
            def _():
                add_to(out_r, k, far_product(t, c))

            r_copy(k).start()

    def left(k):
        t, c = place_of(k)
        late = k >= half

        @pl.when((z > t) & ((z < T - 1) | (k < half)))
        def _():
            out_l[k] = product(t, c).astype(jnp.bfloat16)

            @pl.when((z < T - 2) | ((z == T - 2) & (k < half)))
            def _():
                l_copy(k).wait_recv()
                add_to(out_l, k, in_l[k].astype(jnp.float32))

            @pl.when((z == T - 2) & late)
            def _():
                add_to(out_l, k, far_product(t, c))

            l_copy(k).start()

    def step(k, carry):
        k_r = k - LAG * jnp.maximum(z - 1, 0)
        k_l = k - LAG * jnp.maximum(T - 2 - z, 0)

        def go_right():
            @pl.when((k_r >= 0) & (k_r < 2 * half))
            def _():
                right(k_r)

        def go_left():
            @pl.when((k_l >= 0) & (k_l < 2 * half))
            def _():
                left(k_l)

        @pl.when(z < T // 2)
        def _():
            go_right()
            go_left()

        @pl.when(z >= T // 2)
        def _():
            go_left()
            go_right()

        return carry

    def send_rows(t):
        @pl.when((low & (t > 0)) | (high & (t < T - 1)))
        def _():
            row_copy(t).start()

    early = (T - 1, 0)
    for t in early:
        for s in range(t * per_dest, (t + 1) * per_dest):
            attend(s)
    load_w.wait()
    lax.fori_loop(0, early_chunks, step, 0)
    for t in range(T):
        if t not in early:
            for s in range(t * per_dest, (t + 1) * per_dest):
                attend(s)

    for t in range(T):
        send_rows(t)
    def finish(c, carry):
        cols = pl.ds(pl.multiple_of(c * cw, cw), cw)
        late = c >= early_chunks
        base = c // early_chunks * half + c % early_chunks

        def add_out(more):
            out_ref[:, cols] = (out_ref[:, cols].astype(jnp.float32) + more).astype(jnp.bfloat16)

        out_ref[:, cols] = product(z, c).astype(jnp.bfloat16)

        @pl.when((next_low | next_high) & late)
        def _():
            add_out(far_product(z, c))

        @pl.when((z < T - 2) | ((z == T - 2) & (c < early_chunks)))
        def _():
            k = base + z * early_chunks
            l_copy(k).wait_recv()
            add_out(in_l[k].astype(jnp.float32))

        @pl.when((z > 1) | ((z == 1) & (c < early_chunks)))
        def _():
            k = base + (T - 1 - z) * early_chunks
            r_copy(k).wait_recv()
            add_out(in_r[k].astype(jnp.float32))

        return carry

    lax.fori_loop(early_chunks, half, step, 0)
    lax.fori_loop(0, early_chunks, finish, 0)

    @pl.when(next_low | next_high)
    def _():
        for i in range(1, G // 2):
            owner = lax.rem(me + G - 2 * i, G)
            peer_copy(i, owner).wait_recv()
            pass_copy(i, owner).start()

    @pl.when(next_low | next_high)
    def _():
        for i in range(G // 2):
            pass_copy(i, lax.rem(partner + G - 2 * i, G)).wait_recv()
        for t in range(T):
            @pl.when((next_low & (t > 0)) | (next_high & (t < T - 1)))
            def _():
                row_copy(t).wait_recv()

    lax.fori_loop(half, 2 * half + LAG * (T - 2), step, 0)

    lax.fori_loop(early_chunks, CHUNKS, finish, 0)

    for i in range(1, G):
        q_copy(i, me).wait_send()
    for which in both:
        for i in range(1, G // 2):
            once_copy(which, i, me).wait_send()
        for i in range(G // 2):
            partner_copy(which, i, me).wait_send()

    @pl.when(low | high)
    def _():
        far_copy().wait_send()
        for t in range(T):
            @pl.when((low & (t > 0)) | (high & (t < T - 1)))
            def _():
                row_copy(t).wait_send()

    @pl.when(next_low | next_high)
    def _():
        for i in range(1, G // 2):
            peer_copy(i, me).wait_send()
        for i in range(G // 2):
            pass_copy(i, lax.rem(me + G - 2 * i, G)).wait_send()

    def drain(k, carry):
        n, _ = place_of(k)

        @pl.when((z < T - 1 - n) & ((z > 0) | (k < half)))
        def _():
            r_copy(k).wait_send()

        @pl.when((z > n) & ((z < T - 1) | (k < half)))
        def _():
            l_copy(k).wait_send()

        return carry

    lax.fori_loop(0, 2 * half, drain, 0)


def local(queries, keys, values, lengths, assignment, out_weight):
    G = lax.axis_size("dp")
    T = lax.axis_size("tensor")
    tok_rows, q_width = queries.shape
    n_cols = out_weight.shape[1]
    piece = tok_rows // G
    out_rows = tok_rows // T
    cw = n_cols // CHUNKS
    slots = (T - 1) * CHUNKS
    parts = CHUNKS
    far_cols = CHUNKS // 2 * cw // parts
    att_type = jnp.bfloat16 if piece % 16 == 0 else jnp.float32
    smem = pl.BlockSpec(memory_space=pltpu.SMEM)
    hbm = pl.BlockSpec(memory_space=pl.ANY)
    dma = pltpu.SemaphoreType.DMA
    bf16 = jnp.bfloat16

    def body(*refs):
        kernel(G, T, *refs)

    return pl.pallas_call(
        body,
        out_shape=jax.ShapeDtypeStruct((out_rows, n_cols), bf16),
        in_specs=[smem, smem, hbm, hbm, hbm, hbm],
        out_specs=pl.BlockSpec(memory_space=pltpu.VMEM),
        scratch_shapes=[
            pltpu.VMEM((tok_rows, q_width), bf16),
            pltpu.VMEM((G, piece, q_width), bf16),
            pltpu.VMEM((G, piece, q_width), bf16),
            pltpu.VMEM((G, tok_rows, HD), bf16),
            pltpu.VMEM((G, tok_rows, HD), bf16),
            pltpu.VMEM(out_weight.shape, bf16),
            pltpu.VMEM((tok_rows, q_width), att_type),
            pltpu.VMEM((slots, out_rows, cw), bf16),
            pltpu.VMEM((slots, out_rows, cw), bf16),
            pltpu.VMEM((slots, out_rows, cw), bf16),
            pltpu.VMEM((slots, out_rows, cw), bf16),
            dma, dma, dma((2,)),
            dma((G,)), dma((G,)), dma((G,)), dma((G,)), dma((G,)), dma((G,)),
            dma((slots,)), dma((slots,)), dma((slots,)), dma((slots,)),
            pltpu.VMEM((parts, q_width, far_cols), bf16),
            pltpu.VMEM((tok_rows, q_width), att_type),
            dma, dma, dma((G,)), dma((G,)), dma((T,)), dma((T,)),
        ],
        compiler_params=pltpu.CompilerParams(
            collective_id=0, has_side_effects=True, vmem_limit_bytes=60 << 20
        ),
    )(lengths, assignment, queries, keys, values, out_weight)


def solution(mesh):
    in_specs = (P("dp", "tensor"), P("dp", None), P("dp", None), P(), P(), P("tensor", None))
    out_specs = P(("dp", "tensor"), None)
    return jax.shard_map(local, mesh=mesh, in_specs=in_specs, out_specs=out_specs, check_vma=False)
```
